128 devices in a mesh: member: 8 (over y, core), mesh: 16 (over x, z).
Axes of the slice: x: 4, y: 4, z: 4, core: 2. Of those that a mesh axis runs over, the one named last changes fastest.
Arguments:
- hidden_embedding: bfloat16 [16, 8192, 512], P('member', 'mesh'), may hold values from -6 to 6
- decoder_matrix: bfloat16 [512, 96], replicated, may hold values from -0.25 to 0.25
- baseline_field: float32 [96, 8192], P(None, 'mesh'), may hold values from -6 to 6
- truth_field: float32 [96, 8192], P(None, 'mesh'), may hold values from -6 to 6
- cell_surface_share: float32 [8192], P('mesh'), may hold values from 0.3 to 3
- node_order: int32 [16, 512], P('mesh'), may hold values from 0 to 511, each once within a row
- query: bfloat16 [16, 8192, 512], P('member', 'mesh'), may hold values from -6 to 6
- key_rows: bfloat16 [16, 8192, 512], P('member', 'mesh'), may hold values from -6 to 6
- value_rows: bfloat16 [16, 8192, 512], P('member', 'mesh'), may hold values from -6 to 6
- row_lse: float32 [16, 8, 8192], P('member', None, 'mesh'), may hold values from 6.5 to 8.5
- kv_owner: int32 [16, 16], replicated, may hold values from 0 to 15, each once within a row
- kv_local: int32 [16, 16], replicated, may hold values from 0 to 3
Outputs:
- grad_query: float32 [16, 8192, 512], P('member', 'mesh')
- grad_key: float32 [16, 8192, 512], P('member', 'mesh')
- grad_value: float32 [16, 8192, 512], P('member', 'mesh')
The draws below stay inside these ranges and needn't reach their ends.
Inputs may be any that keep to these rules, and one draw needn't show every extreme that they name: `kv_owner`: each row names every shard once. `node_order`: each row holds every number of 0 to 511 once.
All inputs are finite; a program needn't handle non-finite values.
Results may differ from the reference program's by a relative error of at most 0.0068.
Values may be sent and summed in bfloat16 or wider, within the bound.
No kernel may reach another device: no remote copies, remote signals or barrier semaphores. Data moves between devices by JAX's collectives and lax.ppermute only.
A program may use at most 128 MiB of HBM per device.

```python
import math
import jax
import jax.numpy as jnp
import numpy as np
from jax import lax

CH = 96
HEADS = 8
NODE_DEV = 512
KB = 128
KNB = 16
WIDTH = 512
KBLK_DEV = 4
SHARDS = 16
NODES = 8192
MEMBERS = 16


def with_ends(array, key, low, top_value):
    place = [jax.random.randint(jax.random.fold_in(key, axis), (), 0, length) for axis, length in enumerate(array.shape)]
    longest = array.shape.index(max(array.shape))
    neighbour = place[:longest] + [(place[longest] + 1) % array.shape[longest]] + place[longest + 1:]
    return array.at[tuple(place)].set(low).at[tuple(neighbour)].set(top_value)


def shard_levels(own_key, dims, split, least, high):
    level, own = 1.0, jax.random.fold_in(own_key, 6)
    for axis_at, parts in split:
        heights = jnp.exp(jax.random.uniform(jax.random.fold_in(own, axis_at), (parts,), jnp.float32, least / len(split), high / len(split)))
        level = level * jnp.repeat(heights, dims[axis_at] // parts).reshape([-1 if axis == axis_at else 1 for axis in range(len(dims))])
    return level


def cumulative_ranks(number_of, slope):
    weights = [(1 << 20) // math.isqrt(grade ** slope) + 1 for grade in range(1, number_of + 1)]
    deviation = 1 + sum(weights) // (1 << 30)
    return np.cumsum(np.array([max(1, weight // deviation) for weight in weights]))


def ranked_ids(rng, extent, count, lean):
    listing = cumulative_ranks(count, lean)
    ticket = jax.random.randint(jax.random.fold_in(rng, 1), extent, 0, int(listing[count - 1]))
    grade = jnp.searchsorted(jnp.asarray(listing, jnp.int32), ticket, side="right")
    return jax.random.permutation(jax.random.fold_in(rng, 2), count)[grade].astype(jnp.int32)


def noise(key, shape, width, bound, shards=(), kind=jnp.bfloat16):
    factor_of = shard_levels(key, shape, shards, -0.22, 0.18) if shards else 1.0
    values = jax.random.normal(key, shape, jnp.float32) * width * factor_of
    return jnp.minimum(jnp.maximum(values, -bound), bound).astype(kind)


def setup_inputs(seed: int = 0) -> dict:
    streams_of = jax.random.split(jax.random.key(seed), 13)
    hidden_embedding = noise(streams_of[0], (MEMBERS, NODES, WIDTH), 1.0, 6.0, ((0, 8), (1, 16)))
    decoder_matrix = noise(streams_of[1], (WIDTH, CH), WIDTH ** -0.5, 0.25)
    baseline_field = noise(streams_of[2], (CH, NODES), 1.0, 6.0, ((1, 16),), jnp.float32)
    truth_field = noise(streams_of[3], (CH, NODES), 1.0, 6.0, ((1, 16),), jnp.float32)
    cell_surface_share = jnp.clip(jnp.exp(math.log(3.0) - 2.3025851 * jax.random.uniform(streams_of[4], (NODES,), jnp.float32) ** shard_levels(streams_of[4], (NODES,), ((0, 16),), -0.2, 0.2)), 0.3, 3.0)
    node_order = jax.vmap(lambda own: jax.random.permutation(own, NODE_DEV))(jax.random.split(streams_of[5], SHARDS)).reshape((SHARDS, NODE_DEV)).astype(jnp.int32)
    query = noise(streams_of[6], (MEMBERS, NODES, WIDTH), 1.0, 6.0, ((0, 8), (1, 16)))
    key_rows = noise(streams_of[7], (MEMBERS, NODES, WIDTH), 1.0, 6.0, ((0, 8), (1, 16)))
    value_rows = noise(streams_of[8], (MEMBERS, NODES, WIDTH), 1.0, 6.0, ((0, 8), (1, 16)))
    row_lse = jnp.clip(6.5 + 2.0 * jax.random.uniform(streams_of[9], (MEMBERS, HEADS, NODES), jnp.float32) ** shard_levels(streams_of[9], (MEMBERS, HEADS, NODES), ((0, 8), (2, 16)), -0.2, 0.2), 6.5, 8.5)
    kv_owner = jax.vmap(lambda own: jax.random.permutation(own, SHARDS))(jax.random.split(streams_of[10], SHARDS)).reshape((SHARDS, KNB)).astype(jnp.int32)
    kv_local = with_ends(ranked_ids(streams_of[11], (SHARDS, KNB), KBLK_DEV, 2), jax.random.fold_in(streams_of[11], 3), 0, KBLK_DEV - 1).astype(jnp.int32)
    return {"hidden_embedding": hidden_embedding, "decoder_matrix": decoder_matrix, "baseline_field": baseline_field, "truth_field": truth_field, "cell_surface_share": cell_surface_share, "node_order": node_order, "query": query, "key_rows": key_rows, "value_rows": value_rows, "row_lse": row_lse, "kv_owner": kv_owner, "kv_local": kv_local}


LOSS_SCALE = 4096.0
FAIR_EPS = 0.05
NORM_EPS = 1e-06

def unit_scaled_lines(differences):
    return differences / jnp.sqrt(lax.optimization_barrier(jnp.sum(differences * differences, axis=-2, keepdims=True)) + NORM_EPS)

def outlook_derivative(realization_outlook, truth_field, cell_surface_share):
    realization_list = realization_outlook.shape[0]
    polarity_unit = unit_scaled_lines(realization_outlook - truth_field[None])

    def lone_realization(shard_lines):
        return lax.optimization_barrier(jnp.sum(unit_scaled_lines(shard_lines[None] - realization_outlook), axis=0))
    couple_total = lax.map(lone_realization, realization_outlook)
    weight = LOSS_SCALE * cell_surface_share[None, None, :]
    return weight * (polarity_unit / realization_list - (1.0 - FAIR_EPS) / (realization_list * (realization_list - 1)) * couple_total)

def quantized_entries(numbers):
    return lax.optimization_barrier(numbers.astype(jnp.bfloat16)).astype(jnp.float32)

def tile_grads(queries, grad_rows, log_sums, row_delta, key_tile, value_tile, score_scale):
    scores = jnp.einsum('rhd,khd->hrk', queries, key_tile) * score_scale
    probability = jnp.exp(scores - log_sums[:, :, None])
    dprobs = jnp.einsum('rhd,khd->hrk', grad_rows, value_tile)
    dscores = quantized_entries(probability * (dprobs - row_delta[:, :, None]))
    query_grad = (score_scale * jnp.einsum('hrk,khd->rhd', dscores, key_tile)).astype(jnp.bfloat16)
    key_grad = (score_scale * jnp.einsum('hrk,rhd->khd', dscores, queries)).astype(jnp.bfloat16)
    value_grad = jnp.einsum('hrk,rhd->khd', quantized_entries(probability), grad_rows).astype(jnp.bfloat16)
    return (query_grad, key_grad, value_grad)

def member_grads(arrays, kv_owner, kv_local):
    query, key_rows, value_rows, grad_output, saved_output, row_lse = arrays
    head_count = row_lse.shape[0]
    model_width = query.shape[1]
    head_dim = model_width // head_count
    score_scale = head_dim ** (-0.5)
    split_shape = (SHARDS, NODE_DEV, head_count, head_dim)
    query_blocks = query.astype(jnp.float32).reshape(split_shape)
    grad_blocks = grad_output.astype(jnp.float32).reshape(split_shape)
    saved_blocks = saved_output.astype(jnp.float32).reshape(split_shape)
    row_delta = lax.optimization_barrier(jnp.sum(grad_blocks * saved_blocks, axis=-1)).transpose(0, 2, 1)
    lse_blocks = row_lse.reshape(head_count, SHARDS, NODE_DEV).transpose(1, 0, 2)
    key_blocks = key_rows.astype(jnp.float32).reshape(SHARDS * KBLK_DEV, KB, head_count, head_dim)
    value_blocks = value_rows.astype(jnp.float32).reshape(SHARDS * KBLK_DEV, KB, head_count, head_dim)
    block_ids = (kv_owner * KBLK_DEV + kv_local).astype(jnp.int32)
    zero_grads = jnp.zeros(key_blocks.shape, jnp.float32)

    def per_shard(grads_carry, inputs):
        queries, grad_rows, log_sums, deltas, indices = inputs

        def per_block(running, block_id):
            query_sum, key_grads, value_grads = running
            query_grad, key_grad, value_grad = tile_grads(queries, grad_rows, log_sums, deltas, key_blocks[block_id], value_blocks[block_id], score_scale)
            key_grads = key_grads.at[block_id].add(key_grad.astype(jnp.float32))
            value_grads = value_grads.at[block_id].add(value_grad.astype(jnp.float32))
            return ((query_sum + query_grad.astype(jnp.float32), key_grads, value_grads), None)
        initial = (jnp.zeros(queries.shape, jnp.float32), grads_carry[0], grads_carry[1])
        (query_sum, key_grads, value_grads), unused = lax.scan(per_block, initial, indices)
        return ((key_grads, value_grads), query_sum)
    (key_grads, value_grads), query_sums = lax.scan(per_shard, (zero_grads, zero_grads), (query_blocks, grad_blocks, lse_blocks, row_delta, block_ids))
    return (query_sums.reshape(NODES, model_width), key_grads.reshape(NODES, model_width), value_grads.reshape(NODES, model_width))

def reference(hidden_embedding, decoder_matrix, baseline_field, truth_field, cell_surface_share, node_order, query, key_rows, value_rows, row_lse, kv_owner, kv_local):
    full_coefficient = decoder_matrix.astype(jnp.float32)
    realization_outlook = baseline_field[None] + jnp.einsum('mou,ut->mto', hidden_embedding.astype(jnp.float32), full_coefficient)
    estimate_derivative = quantized_entries(outlook_derivative(realization_outlook, truth_field, cell_surface_share))
    latent_gradient = jnp.einsum('jof,io->jfi', estimate_derivative, full_coefficient).astype(jnp.bfloat16)
    node_index = (node_order + NODE_DEV * jnp.arange(SHARDS, dtype=jnp.int32)[:, None]).reshape(-1).astype(jnp.int32)
    grad_output = jnp.take(latent_gradient, node_index, axis=1)
    saved_output = jnp.take(hidden_embedding, node_index, axis=1)

    def run_member(arrays):
        return member_grads(arrays, kv_owner, kv_local)
    query_grads, key_grads, value_grads = lax.map(run_member, (query, key_rows, value_rows, grad_output, saved_output, row_lse))
    return (query_grads, key_grads, value_grads)
```

```python
import math

import jax
import jax.numpy as jnp
from jax import lax
from jax.experimental import pallas as pl
from jax.experimental.pallas import tpu as pltpu
from jax.sharding import Mesh
from jax.sharding import PartitionSpec as P

KB = 128
SIDE = 4
MEMBER = ("y", "core")
LOSS_SCALE = 4096.0
FAIR_EPS = 0.05
NORM_EPS = 1e-06
LOG2E = math.log2(math.e)
F32 = jnp.float32
BF16 = jnp.bfloat16


def cut_along(x, dim, length):
    dims = x.shape
    tiles = x.reshape(*dims[:dim], length, dims[dim] // length, *dims[dim + 1 :])
    return jnp.moveaxis(tiles, dim, 0)


def in_order(tiles, dim):
    tiles = jnp.moveaxis(tiles, 0, dim)
    dims = tiles.shape
    return tiles.reshape(*dims[:dim], dims[dim] * dims[dim + 1], *dims[dim + 2 :])


def moved_by_axis(tiles, axes, sequence):
    inside = tiles.shape[1:]
    filled = tiles.reshape(*(lax.axis_size(a) for a in axes), *inside)
    for k in sequence:
        filled = lax.all_to_all(filled, axes[k], k, k, tiled=True)
    return filled.reshape(-1, *inside)


def exchange_by_axis(x, axes, sequence, split_dim, concat_dim):
    tiles = cut_along(x, split_dim, lax.axis_size(axes))
    return in_order(moved_by_axis(tiles, axes, sequence), concat_dim)


def unit_scaled_lines(differences):
    return differences / jnp.sqrt(
        jnp.sum(differences * differences, axis=-2, keepdims=True) + NORM_EPS
    )


def outlook_derivative(forecasts, truth_field, cell_surface_share):
    count = forecasts.shape[0]
    polarity_unit = unit_scaled_lines(forecasts - truth_field[None])
    differences = forecasts[:, None] - forecasts[None]
    couple_total = jnp.sum(unit_scaled_lines(differences), axis=1)
    weight = LOSS_SCALE * cell_surface_share[None, None, :]
    return weight * (
        polarity_unit / count - (1.0 - FAIR_EPS) / (count * (count - 1)) * couple_total
    )


def fetched(x, axis, distance):
    return lax.ppermute(x, axis, [(i, (i - distance) % SIDE) for i in range(SIDE)])


def delivered(x, axis, distance):
    return lax.ppermute(x, axis, [(i, (i + distance) % SIDE) for i in range(SIDE)])


def tile_kernel(table, *refs):
    kv = refs[0:4]
    queries = refs[4:8]
    grads = refs[8:12]
    stats = refs[12:16]
    decoder = refs[16]
    dkv = refs[17:21]
    dq = refs[21:25]
    q_stack, g_stack, stat_rows, dk_acc, dv_acc, dq_acc = refs[25:]
    rows = queries[0].shape[0]
    head_dim = 64
    score_scale = head_dim ** (-0.5)
    lane = lax.broadcasted_iota(jnp.int32, (rows, 2 * head_dim), 1)
    first = lane < head_dim
    nt = (((1,), (1,)), ((), ()))
    for t in range(SIDE):
        q = queries[t][...]
        g = lax.dot_general(grads[t][...], decoder[...], nt, preferred_element_type=F32)
        q = q.astype(F32)
        q_stack[t, :rows] = jnp.where(first, q, 0.0).astype(BF16)
        q_stack[t, rows:] = jnp.where(first, 0.0, q).astype(BF16)
        g_stack[t, :rows] = jnp.where(first, g, 0.0).astype(BF16)
        g_stack[t, rows:] = jnp.where(first, 0.0, g).astype(BF16)
        stat_rows[t] = stats[t][0]
    dk_acc[...] = jnp.zeros_like(dk_acc)
    dv_acc[...] = jnp.zeros_like(dv_acc)

    def one_query_block(t, carry):
        q = q_stack[t]
        g = g_stack[t]
        lse = stat_rows[t, 0:1, :] * LOG2E
        delta = stat_rows[t, 1:2, :]
        dq_acc[...] = jnp.zeros_like(dq_acc)
        for pair in ((0, 1), (2, 3)):
            starts = [pl.multiple_of(table[t * SIDE + a] * KB, KB) for a in pair]
            k = jnp.concatenate([kv[a][0, pl.ds(s, KB), :] for a, s in zip(pair, starts)], axis=0)
            v = jnp.concatenate([kv[a][1, pl.ds(s, KB), :] for a, s in zip(pair, starts)], axis=0)
            scores = lax.dot_general(k, q, nt, preferred_element_type=F32)
            p = jnp.exp2(scores * (score_scale * LOG2E) - lse)
            dp = lax.dot_general(v, g, nt, preferred_element_type=F32)
            ds = (p * (dp - delta)).astype(BF16)
            dv = jnp.dot(p.astype(BF16), g, preferred_element_type=F32)
            dk = jnp.dot(ds, q, preferred_element_type=F32)
            for n, (a, s) in enumerate(zip(pair, starts)):
                dv_acc[a, pl.ds(s, KB), :] += dv[n * KB : (n + 1) * KB]
                dk_acc[a, pl.ds(s, KB), :] += dk[n * KB : (n + 1) * KB]
            kt = k.T
            dq_acc[:head_dim] += jnp.dot(kt[:head_dim], ds[:, :rows], preferred_element_type=F32)
            dq_acc[head_dim:] += jnp.dot(kt[head_dim:], ds[:, rows:], preferred_element_type=F32)
        stat_dq = dq_acc[...].T * score_scale
        for n in range(SIDE):

            @pl.when(t == n)
            def _():
                dq[n][...] = stat_dq.astype(dq[n].dtype)

        return carry

    lax.fori_loop(0, SIDE, one_query_block, 0)
    for a in range(SIDE):
        dkv[a][0] = (dk_acc[a] * score_scale).astype(dkv[a].dtype)
        dkv[a][1] = dv_acc[a].astype(dkv[a].dtype)


def attention_tiles(table, kv, queries, grads, stats, decoder_matrix):
    _, rows, width = kv[0].shape
    channels = grads[0].shape[1]
    pairs = width // 128
    kv_spec = pl.BlockSpec((2, rows, 128), lambda h, tab: (0, 0, h))
    q_spec = pl.BlockSpec((rows, 128), lambda h, tab: (0, h))
    g_spec = pl.BlockSpec((rows, channels), lambda h, tab: (0, 0))
    s_spec = pl.BlockSpec((1, 2, 2 * rows), lambda h, tab: (h, 0, 0))
    d_spec = pl.BlockSpec((128, channels), lambda h, tab: (h, 0))
    kinds = [F32, BF16, BF16, BF16]
    out = pl.pallas_call(
        tile_kernel,
        out_shape=[jax.ShapeDtypeStruct((2, rows, width), d) for d in kinds]
        + [jax.ShapeDtypeStruct((rows, width), d) for d in kinds],
        grid_spec=pltpu.PrefetchScalarGridSpec(
            num_scalar_prefetch=1,
            grid=(pairs,),
            in_specs=[kv_spec] * 4 + [q_spec] * 4 + [g_spec] * 4 + [s_spec] * 4 + [d_spec],
            out_specs=[kv_spec] * 4 + [q_spec] * 4,
            scratch_shapes=[
                pltpu.VMEM((SIDE, 2 * rows, 128), BF16),
                pltpu.VMEM((SIDE, 2 * rows, 128), BF16),
                pltpu.VMEM((SIDE, 2, 2 * rows), F32),
                pltpu.VMEM((SIDE, rows, 128), F32),
                pltpu.VMEM((SIDE, rows, 128), F32),
                pltpu.VMEM((128, rows), F32),
            ],
        ),
        compiler_params=pltpu.CompilerParams(
            dimension_semantics=("arbitrary",), vmem_limit_bytes=48 * 1024 * 1024
        ),
        name="attention_tiles",
    )(table, *kv, *queries, *grads, *stats, decoder_matrix)
    return out[:4], out[4:]


def shards(
    hidden_embedding,
    decoder_matrix,
    baseline_field,
    truth_field,
    cell_surface_share,
    node_order,
    query,
    key_rows,
    value_rows,
    row_lse,
    kv_owner,
    kv_local,
):
    members, nodes, width = hidden_embedding.shape
    heads = row_lse.shape[1]
    pairs = heads // 2
    x_at = lax.axis_index("x")
    z_at = lax.axis_index("z")
    around = jnp.arange(SIDE, dtype=jnp.int32)
    axes = (("x", "z"), ("z", "x"))

    shard_ids = jnp.arange(kv_owner.shape[0], dtype=jnp.int32)
    where = jnp.sum(
        jnp.where(kv_owner[:, :, None] == shard_ids[None, None, :], kv_local[:, :, None], 0), axis=1
    )
    tables = []
    for key_axis, query_axis in axes:
        if key_axis == "x":
            s_ids = x_at * SIDE + (z_at + around) % SIDE
            o_ids = ((x_at + around) % SIDE) * SIDE + z_at
        else:
            s_ids = ((x_at + around) % SIDE) * SIDE + z_at
            o_ids = x_at * SIDE + (z_at + around) % SIDE
        tables.append(where[s_ids][:, o_ids].reshape(-1))

    kv, queries = [], []
    for m, (key_axis, query_axis) in enumerate(axes):
        own = jnp.stack([key_rows[m], value_rows[m]])
        kv.append([own] + [fetched(own, key_axis, d) for d in (1, 2, 3)])
        own = query[m]
        queries.append([own] + [fetched(own, query_axis, d) for d in (1, 2, 3)])

    forecast = baseline_field[None] + jnp.einsum(
        "mou,ut->mto", hidden_embedding, decoder_matrix, preferred_element_type=F32
    )
    groups = lax.axis_size(MEMBER)
    member_index = lax.axis_index(MEMBER)
    everyone = exchange_by_axis(forecast, MEMBER, (1, 0), 2, 0)
    span = nodes // groups
    offset = member_index * span
    observed = lax.dynamic_slice_in_dim(truth_field, offset, span, 1)
    area = lax.dynamic_slice_in_dim(cell_surface_share, offset, span, 0)
    derivative = outlook_derivative(everyone, observed, area).astype(BF16)
    grad_forecast = exchange_by_axis(derivative, MEMBER, (1, 0), 0, 2)

    permuter = (node_order[0][:, None] == jnp.arange(nodes, dtype=jnp.int32)[None, :]).astype(BF16)
    grad_rows = jnp.einsum(
        "mcg,tg->mtc", grad_forecast, permuter, preferred_element_type=F32
    ).astype(BF16)
    grad_latent = jnp.einsum(
        "wc,mtc->mwt", decoder_matrix, grad_rows, preferred_element_type=F32
    ).astype(BF16)
    saved = jnp.einsum("mgw,tg->mwt", hidden_embedding, permuter, preferred_element_type=F32).astype(
        BF16
    )
    split = (members, heads, width // heads, nodes)
    delta = jnp.sum(
        grad_latent.astype(F32).reshape(split) * saved.astype(F32).reshape(split), axis=2
    )
    stats = jnp.stack(
        [row_lse.reshape(members, pairs, 2 * nodes), delta.reshape(members, pairs, 2 * nodes)], axis=2
    )

    key_parts, query_parts = [], []
    for m, (key_axis, query_axis) in enumerate(axes):
        own_g, own_s = grad_rows[m], stats[m]
        grads = [own_g] + [fetched(own_g, query_axis, d) for d in (1, 2, 3)]
        stat = [own_s] + [fetched(own_s, query_axis, d) for d in (1, 2, 3)]
        dkv, dq = attention_tiles(tables[m], kv[m], queries[m], grads, stat, decoder_matrix)
        back = dkv[0]
        for d in (1, 2, 3):
            back = back + delivered(dkv[d], key_axis, d).astype(F32)
        key_parts.append(back)
        back = dq[0]
        for d in (1, 2, 3):
            back = back + delivered(dq[d], query_axis, d).astype(F32)
        query_parts.append(back)
    grad_query = jnp.stack(query_parts)
    grad_key = jnp.stack([k[0] for k in key_parts])
    grad_value = jnp.stack([k[1] for k in key_parts])
    return grad_query, grad_key, grad_value


def solution(mesh):
    finer = Mesh(mesh.devices.reshape(4, 2, SIDE, SIDE), ("y", "core", "x", "z"))
    plane = ("x", "z")
    in_specs = (
        P(MEMBER, plane, None),
        P(),
        P(None, plane),
        P(None, plane),
        P(plane),
        P(plane, None),
        P(MEMBER, plane, None),
        P(MEMBER, plane, None),
        P(MEMBER, plane, None),
        P(MEMBER, None, plane),
        P(),
        P(),
    )
    out_specs = (P(MEMBER, plane, None), P(MEMBER, plane, None), P(MEMBER, plane, None))
    return jax.shard_map(
        shards, mesh=finer, in_specs=in_specs, out_specs=out_specs, check_vma=False
    )
```

```python
import functools
import math

import jax
import jax.numpy as jnp
from jax import lax
from jax.experimental import pallas as pl
from jax.experimental.pallas import tpu as pltpu
from jax.sharding import Mesh
from jax.sharding import PartitionSpec as P

KB = 128
SIDE = 4
MEMBER = ("y", "core")
LOSS_SCALE = 4096.0
FAIR_EPS = 0.05
NORM_EPS = 1e-06
LOG2E = math.log2(math.e)
F32 = jnp.float32
BF16 = jnp.bfloat16


def cut_along(x, dim, length):
    dims = x.shape
    tiles = x.reshape(*dims[:dim], length, dims[dim] // length, *dims[dim + 1 :])
    return jnp.moveaxis(tiles, dim, 0)


def in_order(tiles, dim):
    tiles = jnp.moveaxis(tiles, 0, dim)
    dims = tiles.shape
    return tiles.reshape(*dims[:dim], dims[dim] * dims[dim + 1], *dims[dim + 2 :])


def moved_by_axis(tiles, axes, sequence):
    inside = tiles.shape[1:]
    filled = tiles.reshape(*(lax.axis_size(a) for a in axes), *inside)
    for k in sequence:
        filled = lax.all_to_all(filled, axes[k], k, k, tiled=True)
    return filled.reshape(-1, *inside)


def exchange_by_axis(x, axes, sequence, split_dim, concat_dim):
    tiles = cut_along(x, split_dim, lax.axis_size(axes))
    return in_order(moved_by_axis(tiles, axes, sequence), concat_dim)


def unit_scaled_lines(differences):
    return differences / jnp.sqrt(
        jnp.sum(differences * differences, axis=-2, keepdims=True) + NORM_EPS
    )


def outlook_derivative(forecasts, truth_field, cell_surface_share):
    count = forecasts.shape[0]
    polarity_unit = unit_scaled_lines(forecasts - truth_field[None])
    differences = forecasts[:, None] - forecasts[None]
    couple_total = jnp.sum(unit_scaled_lines(differences), axis=1)
    weight = LOSS_SCALE * cell_surface_share[None, None, :]
    return weight * (
        polarity_unit / count - (1.0 - FAIR_EPS) / (count * (count - 1)) * couple_total
    )


def fetched(x, axis, distance):
    return lax.ppermute(x, axis, [(i, (i - distance) % SIDE) for i in range(SIDE)])


def delivered(x, axis, distance):
    return lax.ppermute(x, axis, [(i, (i + distance) % SIDE) for i in range(SIDE)])


def head_pair_tiles(table, base, kv, queries, lates, decoder, out, scratch):
    q_stack, g_stack, stat_rows, dk_acc, dv_acc, dq_acc = scratch
    rows = q_stack.shape[1] // 2
    channels = decoder.shape[1]
    head = pl.program_id(0) * 2 + base
    head_dim = 64
    score_scale = head_dim ** (-0.5)
    lane = lax.broadcasted_iota(jnp.int32, (rows, 2 * head_dim), 1)
    first = lane < head_dim
    nt = (((1,), (1,)), ((), ()))
    tn = (((0,), (1,)), ((), ()))
    for t in range(SIDE):
        q = queries[t][...].astype(F32)
        g = lax.dot_general(
            lates[t][:channels, :].astype(BF16), decoder[...], tn, preferred_element_type=F32
        )
        q_stack[t, :rows] = jnp.where(first, q, 0.0).astype(BF16)
        q_stack[t, rows:] = jnp.where(first, 0.0, q).astype(BF16)
        g_stack[t, :rows] = jnp.where(first, g, 0.0).astype(BF16)
        g_stack[t, rows:] = jnp.where(first, 0.0, g).astype(BF16)
        for n in range(2):
            stat_rows[t, n : n + 1, :rows] = lates[t][pl.ds(channels + 8 * n + head, 1), :]
            stat_rows[t, n : n + 1, rows:] = lates[t][pl.ds(channels + 8 * n + head + 1, 1), :]
    dk_acc[...] = jnp.zeros_like(dk_acc)
    dv_acc[...] = jnp.zeros_like(dv_acc)

    def one_query_block(t, carry):
        q = q_stack[t]
        g = g_stack[t]
        lse = stat_rows[t, 0:1, :] * LOG2E
        delta = stat_rows[t, 1:2, :]
        dq_acc[...] = jnp.zeros_like(dq_acc)
        for pair in ((0, 1), (2, 3)):
            starts = [pl.multiple_of(table[t * SIDE + a] * KB, KB) for a in pair]
            k = jnp.concatenate([kv[a][0][pl.ds(s, KB), :] for a, s in zip(pair, starts)], axis=0)
            v = jnp.concatenate([kv[a][1][pl.ds(s, KB), :] for a, s in zip(pair, starts)], axis=0)
            scores = lax.dot_general(k, q, nt, preferred_element_type=F32)
            p = jnp.exp2(scores * (score_scale * LOG2E) - lse)
            dp = lax.dot_general(v, g, nt, preferred_element_type=F32)
            ds = (p * (dp - delta)).astype(BF16)
            dv = jnp.dot(p.astype(BF16), g, preferred_element_type=F32)
            dk = jnp.dot(ds, q, preferred_element_type=F32)
            for n, (a, s) in enumerate(zip(pair, starts)):
                dv_acc[a, pl.ds(s, KB), :] += dv[n * KB : (n + 1) * KB]
                dk_acc[a, pl.ds(s, KB), :] += dk[n * KB : (n + 1) * KB]
            kt = k.T
            dq_acc[:head_dim] += jnp.dot(kt[:head_dim], ds[:, :rows], preferred_element_type=F32)
            dq_acc[head_dim:] += jnp.dot(kt[head_dim:], ds[:, rows:], preferred_element_type=F32)
        dq = dq_acc[...].T * score_scale
        for n in range(SIDE):

            @pl.when(t == n)
            def _():
                out(2, n, dq)

        return carry

    lax.fori_loop(0, SIDE, one_query_block, 0)
    for a in range(SIDE):
        out(0, a, dk_acc[a] * score_scale)
        out(1, a, dv_acc[a])


def tile_kernel(table, *refs, base):
    key_own, value_own, query_own, late_own, decoder = refs[0:5]
    fetch_x, fetch_z = refs[5:8], refs[8:11]
    late_x, late_z = refs[11:14], refs[14:17]
    own_out = refs[17]
    send_x, send_z = refs[18:21], refs[21:24]
    scratch = refs[24:]
    sides = ((fetch_x, send_x, late_x), (fetch_z, send_z, late_z))
    for m in range(2):
        key_fetch, key_send, _ = sides[m]
        query_fetch, query_send, late = sides[1 - m]
        kv = [(key_own.at[m], value_own.at[m])] + [(r.at[0], r.at[1]) for r in key_fetch]
        queries = [query_own.at[m]] + [r.at[2] for r in query_fetch]
        lates = [late_own.at[m]] + list(late)

        def out(kind, n, value, m=m, key_send=key_send, query_send=query_send):
            if n == 0:
                own_out[kind, m] = value
            else:
                ref = (query_send if kind == 2 else key_send)[n - 1]
                ref[kind] = value.astype(BF16)

        head_pair_tiles(
            table.at[m], base, kv, queries, lates, decoder, out, scratch
        )


def attention_tiles(half, tables, key_rows, value_rows, query, fetched_x, fetched_z, late_own, late_x, late_z, decoder_matrix):
    members, rows, width = key_rows.shape
    stats, channels = late_own.shape[1], decoder_matrix.shape[1]
    pairs = width // 256
    base = half * pairs
    own_spec = pl.BlockSpec((members, rows, 128), lambda h, tab: (0, 0, base + h))
    near_spec = pl.BlockSpec((None, 3, rows, 128), lambda h, tab: (half, 0, 0, h))
    far_spec = pl.BlockSpec((3, rows, 128), lambda h, tab: (0, 0, h))
    fetch_specs = [near_spec, far_spec, near_spec]
    late_spec = pl.BlockSpec((stats, rows), lambda h, tab: (0, 0))
    out = pl.pallas_call(
        functools.partial(tile_kernel, base=2 * base),
        out_shape=[jax.ShapeDtypeStruct((3, members, rows, width // 2), F32)]
        + [jax.ShapeDtypeStruct((3, rows, width // 2), BF16)] * 6,
        grid_spec=pltpu.PrefetchScalarGridSpec(
            num_scalar_prefetch=1,
            grid=(pairs,),
            in_specs=[own_spec] * 3
            + [
                pl.BlockSpec((members, stats, rows), lambda h, tab: (0, 0, 0)),
                pl.BlockSpec((128, channels), lambda h, tab: (base + h, 0)),
            ]
            + fetch_specs * 2
            + [late_spec] * 6,
            out_specs=[pl.BlockSpec((3, members, rows, 128), lambda h, tab: (0, 0, 0, h))]
            + [far_spec] * 6,
            scratch_shapes=[
                pltpu.VMEM((SIDE, 2 * rows, 128), BF16),
                pltpu.VMEM((SIDE, 2 * rows, 128), BF16),
                pltpu.VMEM((SIDE, 2, 2 * rows), F32),
                pltpu.VMEM((SIDE, rows, 128), F32),
                pltpu.VMEM((SIDE, rows, 128), F32),
                pltpu.VMEM((128, rows), F32),
            ],
        ),
        compiler_params=pltpu.CompilerParams(
            dimension_semantics=("arbitrary",), vmem_limit_bytes=50 * 1024 * 1024
        ),
        name="attention_tiles",
    )(tables, key_rows, value_rows, query, late_own, decoder_matrix, *fetched_x, *fetched_z, *late_x, *late_z)
    return out[0], out[1:4], out[4:7]


def sum_kernel(*refs):
    own = refs[0]
    got_x, got_z = refs[1:4], refs[4:7]
    outs = refs[-3:]
    for kind, ref in enumerate(outs):
        for m in range(2):
            got = (got_x, got_z)[m if kind < 2 else 1 - m]
            total = own[kind, m]
            for g in got:
                total = total + g[kind].astype(F32)
            ref[m] = total


def summed(half, own, got_x, got_z, outs):
    _, members, rows, lanes = own.shape
    grid = (2,)
    own_spec = pl.BlockSpec((3, members, rows // 2, lanes), lambda r: (0, 0, r, 0))
    got_spec = pl.BlockSpec((3, rows // 2, lanes), lambda r: (0, r, 0))
    out_spec = pl.BlockSpec((members, rows // 2, lanes), lambda r: (0, r, half))
    shape = jax.ShapeDtypeStruct((members, rows, 2 * lanes), F32)
    kept = list(outs) if outs else []
    return pl.pallas_call(
        sum_kernel,
        out_shape=[shape] * 3,
        grid=grid,
        in_specs=[own_spec] + [got_spec] * 6 + [pl.BlockSpec(memory_space=pl.ANY)] * len(kept),
        out_specs=[out_spec] * 3,
        input_output_aliases={7 + n: n for n in range(len(kept))},
        compiler_params=pltpu.CompilerParams(vmem_limit_bytes=50 * 1024 * 1024),
        name="summed",
    )(own, *got_x, *got_z, *kept)


def ring_fetched(own, axis):
    after, before = fetched(own, axis, 1), fetched(own, axis, 3)
    return after, (fetched(after[0], axis, 1), fetched(before[1], axis, 3)), before


def outgoing(keys, values, queries):
    stacked = jnp.stack([keys, values, queries])
    kinds, rows, width = stacked.shape
    return jnp.stack([stacked[..., : width // 2], stacked[..., width // 2 :]])


def shards(
    hidden_embedding,
    decoder_matrix,
    baseline_field,
    truth_field,
    cell_surface_share,
    node_order,
    query,
    key_rows,
    value_rows,
    row_lse,
    kv_owner,
    kv_local,
):
    members, nodes, width = hidden_embedding.shape
    heads = row_lse.shape[1]
    x_at = lax.axis_index("x")
    z_at = lax.axis_index("z")

    x_after, x_far, x_before = ring_fetched(outgoing(key_rows[0], value_rows[0], query[1]), "x")
    z_after, z_far, z_before = ring_fetched(outgoing(key_rows[1], value_rows[1], query[0]), "z")

    forecast = baseline_field[None] + jnp.einsum(
        "mou,ut->mto", hidden_embedding, decoder_matrix, preferred_element_type=F32
    )
    groups = lax.axis_size(MEMBER)
    member_index = lax.axis_index(MEMBER)
    everyone = exchange_by_axis(forecast, MEMBER, (1, 0), 2, 0)
    span = nodes // groups
    offset = member_index * span
    observed = lax.dynamic_slice_in_dim(truth_field, offset, span, 1)
    area = lax.dynamic_slice_in_dim(cell_surface_share, offset, span, 0)
    derivative = outlook_derivative(everyone, observed, area).astype(BF16)
    grad_forecast = exchange_by_axis(derivative, MEMBER, (1, 0), 0, 2)

    shard_ids = jnp.arange(SIDE * SIDE, dtype=jnp.int32)
    around = jnp.arange(SIDE, dtype=jnp.int32)
    named = jnp.sum(
        jnp.where(kv_owner[:, :, None] == shard_ids[None, None, :], kv_local[:, :, None], 0), axis=1
    ).reshape(SIDE, SIDE, SIDE, SIDE)
    x_near = ((x_at + around) % SIDE)[:, None] == around[None, :]
    z_near = ((z_at + around) % SIDE)[:, None] == around[None, :]
    x_here, z_here = x_near[0], z_near[0]

    def picked(sx, sz, ox, oz):
        chosen = (
            sx[:, None, None, None, :, None, None, None]
            & sz[None, :, None, None, None, :, None, None]
            & ox[None, None, :, None, None, None, :, None]
            & oz[None, None, None, :, None, None, None, :]
        )
        return jnp.sum(jnp.where(chosen, named, 0), axis=(4, 5, 6, 7)).reshape(-1)

    tables = jnp.stack(
        [
            picked(x_here[None], z_near, x_near, z_here[None]),
            picked(x_near, z_here[None], x_here[None], z_near),
        ]
    )

    permuter = (node_order[0][:, None] == jnp.arange(nodes, dtype=jnp.int32)[None, :]).astype(BF16)
    grad_columns = jnp.einsum(
        "mcg,tg->mct", grad_forecast, permuter, preferred_element_type=F32
    )
    grad_latent = jnp.einsum(
        "wc,mct->mwt", decoder_matrix, grad_columns.astype(BF16), preferred_element_type=F32
    ).astype(BF16)
    saved = jnp.einsum("mgw,tg->mwt", hidden_embedding, permuter, preferred_element_type=F32).astype(
        BF16
    )
    split = (members, heads, width // heads, nodes)
    delta = jnp.sum(
        grad_latent.astype(F32).reshape(split) * saved.astype(F32).reshape(split), axis=2
    )
    late_own = jnp.concatenate([grad_columns, row_lse, delta], axis=1)
    late_z = [fetched(late_own[0], "z", d) for d in (1, 2, 3)]
    late_x = [fetched(late_own[1], "x", d) for d in (1, 2, 3)]

    outs = None
    parts = []
    for half in range(2):
        own, send_x, send_z = attention_tiles(
            half,
            tables,
            key_rows,
            value_rows,
            query,
            (x_after, x_far[half], x_before),
            (z_after, z_far[half], z_before),
            late_own,
            late_x,
            late_z,
            decoder_matrix,
        )
        got_x = [delivered(send_x[d - 1], "x", d) for d in (1, 2, 3)]
        got_z = [delivered(send_z[d - 1], "z", d) for d in (1, 2, 3)]
        parts.append((own, got_x, got_z))
    for half, (own, got_x, got_z) in enumerate(parts):
        outs = summed(half, own, got_x, got_z, outs)
    grad_key, grad_value, grad_query = outs
    return grad_query, grad_key, grad_value


def solution(mesh):
    finer = Mesh(mesh.devices.reshape(4, 2, SIDE, SIDE), ("y", "core", "x", "z"))
    plane = ("x", "z")
    in_specs = (
        P(MEMBER, plane, None),
        P(),
        P(None, plane),
        P(None, plane),
        P(plane),
        P(plane, None),
        P(MEMBER, plane, None),
        P(MEMBER, plane, None),
        P(MEMBER, plane, None),
        P(MEMBER, None, plane),
        P(),
        P(),
    )
    out_specs = (P(MEMBER, plane, None), P(MEMBER, plane, None), P(MEMBER, plane, None))
    return jax.shard_map(
        shards, mesh=finer, in_specs=in_specs, out_specs=out_specs, check_vma=False
    )
```

```python
import functools
import math

import jax
import jax.numpy as jnp
from jax import lax
from jax.experimental import pallas as pl
from jax.experimental.pallas import tpu as pltpu
from jax.sharding import Mesh
from jax.sharding import PartitionSpec as P

KB = 128
SIDE = 4
MEMBER = ("y", "core")
LOSS_SCALE = 4096.0
FAIR_EPS = 0.05
NORM_EPS = 1e-06
LOG2E = math.log2(math.e)
F32 = jnp.float32
BF16 = jnp.bfloat16


def score_kernel(forecast_ref, truth_ref, area_ref, out_ref):
    groups, _, lanes = forecast_ref.shape
    count = 2 * groups
    swapped = [pltpu.roll(forecast_ref[j], lanes // 2, 1) for j in range(groups)]

    def unit(x):
        return x * (1.0 / jnp.sqrt(jnp.sum(x * x, axis=0, keepdims=True) + NORM_EPS))

    weight = LOSS_SCALE * area_ref[...]
    for j in range(groups):
        one = forecast_ref[j]
        total = unit(one - swapped[j])
        for k in range(groups):
            if k != j:
                total = total + unit(one - forecast_ref[k]) + unit(one - swapped[k])
        gradient = weight * (
            unit(one - truth_ref[...]) / count - (1.0 - FAIR_EPS) / (count * (count - 1)) * total
        )
        out_ref[j] = gradient.astype(BF16)


def score_gradient(forecasts, truth, area):
    return pl.pallas_call(
        score_kernel, out_shape=jax.ShapeDtypeStruct(forecasts.shape, BF16), name="score_gradient"
    )(forecasts, truth, area)


def two_parts(x):
    high = x.astype(BF16)
    return [high, (x - lax.reduce_precision(x, 8, 7)).astype(BF16)]


def fetched(x, axis, distance):
    return lax.ppermute(x, axis, [(i, (i - distance) % SIDE) for i in range(SIDE)])


def delivered(x, axis, distance):
    return lax.ppermute(x, axis, [(i, (i + distance) % SIDE) for i in range(SIDE)])


def head_pair_tiles(table, base, kv, queries, lates, decoder, out, scratch):
    q_stack, g_stack, stat_rows, joined, dk_acc, dv_acc, dq_acc = scratch
    rows = q_stack.shape[1] // 2
    channels = decoder.shape[1]
    head = pl.program_id(0) * 2 + base
    head_dim = 64
    score_scale = head_dim ** (-0.5)
    lane = lax.broadcasted_iota(jnp.int32, (rows, 2 * head_dim), 1)
    first = lane < head_dim
    nt = (((1,), (1,)), ((), ()))
    tn = (((0,), (1,)), ((), ()))
    for t in range(SIDE):
        q = queries[t][...].astype(F32)
        g = lax.dot_general(
            lates[t][:channels, :], decoder[...], tn, preferred_element_type=F32
        )
        q_stack[t, :rows] = jnp.where(first, q, 0.0).astype(BF16)
        q_stack[t, rows:] = jnp.where(first, 0.0, q).astype(BF16)
        g_stack[t, :rows] = jnp.where(first, g, 0.0).astype(BF16)
        g_stack[t, rows:] = jnp.where(first, 0.0, g).astype(BF16)
        stat = lates[t][channels:, :].astype(F32)
        joined[: stat.shape[0] // 2] = stat[: stat.shape[0] // 2] + stat[stat.shape[0] // 2 :]
        for n in range(2):
            stat_rows[t, n : n + 1, :rows] = joined[pl.ds(8 * n + head, 1), :]
            stat_rows[t, n : n + 1, rows:] = joined[pl.ds(8 * n + head + 1, 1), :]
    dk_acc[...] = jnp.zeros_like(dk_acc)
    dv_acc[...] = jnp.zeros_like(dv_acc)

    def one_query_block(t, carry):
        q = q_stack[t]
        g = g_stack[t]
        lse = stat_rows[t, 0:1, :] * LOG2E
        delta = stat_rows[t, 1:2, :]
        dq_acc[...] = jnp.zeros_like(dq_acc)
        for pair in ((0, 1), (2, 3)):
            starts = [pl.multiple_of(table[t * SIDE + a] * KB, KB) for a in pair]
            k = jnp.concatenate([kv[a][0][pl.ds(s, KB), :] for a, s in zip(pair, starts)], axis=0)
            v = jnp.concatenate([kv[a][1][pl.ds(s, KB), :] for a, s in zip(pair, starts)], axis=0)
            scores = lax.dot_general(k, q, nt, preferred_element_type=F32)
            p = jnp.exp2(scores * (score_scale * LOG2E) - lse)
            dp = lax.dot_general(v, g, nt, preferred_element_type=F32)
            ds = (p * (dp - delta)).astype(BF16)
            dv = jnp.dot(p.astype(BF16), g, preferred_element_type=F32)
            dk = jnp.dot(ds, q, preferred_element_type=F32)
            for n, (a, s) in enumerate(zip(pair, starts)):
                dv_acc[a, pl.ds(s, KB), :] += dv[n * KB : (n + 1) * KB]
                dk_acc[a, pl.ds(s, KB), :] += dk[n * KB : (n + 1) * KB]
            kt = k.T
            dq_acc[:head_dim] += jnp.dot(kt[:head_dim], ds[:, :rows], preferred_element_type=F32)
            dq_acc[head_dim:] += jnp.dot(kt[head_dim:], ds[:, rows:], preferred_element_type=F32)
        dq = dq_acc[...].T * score_scale
        for n in range(SIDE):

            @pl.when(t == n)
            def _():
                out(2, n, dq)

        return carry

    lax.fori_loop(0, SIDE, one_query_block, 0)
    for a in range(SIDE):
        out(0, a, dk_acc[a] * score_scale)
        out(1, a, dv_acc[a])


def tile_kernel(table, *refs, base):
    key_own, value_own, query_own, late_own, decoder = refs[0:5]
    fetch_x, fetch_z = refs[5:8], refs[8:11]
    late_x, late_z = refs[11:14], refs[14:17]
    send_x, own_z, send_z = refs[17], refs[18], refs[19:22]
    scratch = refs[22:]
    sides = ((fetch_x, late_x), (fetch_z, late_z))
    for m in range(2):
        key_fetch = sides[m][0]
        query_fetch, late = sides[1 - m]
        kv = [(key_own.at[m], value_own.at[m])] + [(r.at[0], r.at[1]) for r in key_fetch]
        queries = [query_own.at[m]] + [r.at[2] for r in query_fetch]
        lates = [late_own.at[m]] + list(late)

        def out(kind, n, value, m=m):
            if m == (1 if kind == 2 else 0):
                send_x[table[2, n], kind] = value.astype(BF16)
            elif n == 0:
                own_z[kind] = value
            else:
                send_z[n - 1][kind] = value.astype(BF16)

        head_pair_tiles(
            table.at[m], base, kv, queries, lates, decoder, out, scratch
        )


def attention_tiles(half, tables, key_rows, value_rows, query, fetched_x, fetched_z, late_own, late_x, late_z, decoder_matrix):
    members, rows, width = key_rows.shape
    stats, channels = late_own.shape[1], decoder_matrix.shape[1]
    pairs = width // 256
    base = half * pairs
    own_spec = pl.BlockSpec((members, rows, 128), lambda h, tab: (0, 0, base + h))
    near_spec = pl.BlockSpec((None, 3, rows, 128), lambda h, tab: (half, 0, 0, h))
    once_spec = pl.BlockSpec((None, 3, rows, 128), lambda h, tab: (0, 0, 0, h))
    far_spec = pl.BlockSpec((3, rows, 128), lambda h, tab: (0, 0, h))
    fetch_specs = [near_spec, once_spec, near_spec]
    late_spec = pl.BlockSpec((stats, rows), lambda h, tab: (0, 0))
    out = pl.pallas_call(
        functools.partial(tile_kernel, base=2 * base),
        out_shape=[
            jax.ShapeDtypeStruct((SIDE, 3, rows, width // 2), BF16),
            jax.ShapeDtypeStruct((3, rows, width // 2), F32),
        ]
        + [jax.ShapeDtypeStruct((3, rows, width // 2), BF16)] * 3,
        grid_spec=pltpu.PrefetchScalarGridSpec(
            num_scalar_prefetch=1,
            grid=(pairs,),
            in_specs=[own_spec] * 3
            + [
                pl.BlockSpec((members, stats, rows), lambda h, tab: (0, 0, 0)),
                pl.BlockSpec((128, channels), lambda h, tab: (base + h, 0)),
            ]
            + fetch_specs * 2
            + [late_spec] * 6,
            out_specs=[pl.BlockSpec((SIDE, 3, rows, 128), lambda h, tab: (0, 0, 0, h))]
            + [far_spec] * 4,
            scratch_shapes=[
                pltpu.VMEM((SIDE, 2 * rows, 128), BF16),
                pltpu.VMEM((SIDE, 2 * rows, 128), BF16),
                pltpu.VMEM((SIDE, 2, 2 * rows), F32),
                pltpu.VMEM((16, rows), F32),
                pltpu.VMEM((SIDE, rows, 128), F32),
                pltpu.VMEM((SIDE, rows, 128), F32),
                pltpu.VMEM((128, rows), F32),
            ],
        ),
        compiler_params=pltpu.CompilerParams(
            dimension_semantics=("arbitrary",), vmem_limit_bytes=50 * 1024 * 1024
        ),
        cost_estimate=pl.CostEstimate(
            flops=5 * 2 * (SIDE * SIDE * KB) * rows * 128 * 4 * pairs * members,
            transcendentals=SIDE * SIDE * KB * rows * 2 * pairs * members,
            bytes_accessed=20 * 1024 * 1024,
        ),
        name="attention_tiles",
    )(tables, key_rows, value_rows, query, late_own, decoder_matrix, *fetched_x, *fetched_z, *late_x, *late_z)
    return out[0], out[1], out[2:]


def sum_kernel(got_x, own_z, *refs):
    got_z, outs = refs[:3], refs[-3:]
    for kind, ref in enumerate(outs):
        along_x = got_x[0, kind].astype(F32)
        for n in range(1, SIDE):
            along_x = along_x + got_x[n, kind].astype(F32)
        along_z = own_z[kind]
        for got in got_z:
            along_z = along_z + got[kind].astype(F32)
        ref[1 if kind == 2 else 0] = along_x
        ref[0 if kind == 2 else 1] = along_z


def summed(half, got_x, own_z, got_z, outs):
    _, rows, lanes = own_z.shape
    z_spec = pl.BlockSpec((3, rows // 2, lanes), lambda r: (0, r, 0))
    shape = jax.ShapeDtypeStruct((2, rows, 2 * lanes), F32)
    kept = list(outs) if outs else []
    return pl.pallas_call(
        sum_kernel,
        out_shape=[shape] * 3,
        grid=(2,),
        in_specs=[pl.BlockSpec((SIDE, 3, rows // 2, lanes), lambda r: (0, 0, r, 0))]
        + [z_spec] * 4
        + [pl.BlockSpec(memory_space=pl.ANY)] * len(kept),
        out_specs=[pl.BlockSpec((2, rows // 2, lanes), lambda r: (0, r, half))] * 3,
        input_output_aliases={5 + n: n for n in range(len(kept))},
        compiler_params=pltpu.CompilerParams(vmem_limit_bytes=50 * 1024 * 1024),
        name="summed",
    )(got_x, own_z, *got_z, *kept)


def ring_far(after, before, axis):
    return fetched(after[0:1], axis, 1), fetched(before[1:2], axis, 3)


def outgoing(keys, values, queries):
    stacked = jnp.stack([keys, values, queries])
    kinds, rows, width = stacked.shape
    return jnp.stack([stacked[..., : width // 2], stacked[..., width // 2 :]])


def shards(
    hidden_embedding,
    decoder_matrix,
    baseline_field,
    truth_field,
    cell_surface_share,
    node_order,
    query,
    key_rows,
    value_rows,
    row_lse,
    kv_owner,
    kv_local,
):
    members, nodes, width = hidden_embedding.shape
    heads = row_lse.shape[1]
    x_at = lax.axis_index("x")
    z_at = lax.axis_index("z")

    own_x = outgoing(key_rows[0], value_rows[0], query[1])
    own_z = outgoing(key_rows[1], value_rows[1], query[0])
    near = [fetched(own_x, "x", 1), fetched(own_x, "x", 3), fetched(own_z, "z", 1), fetched(own_z, "z", 3)]

    forecast = baseline_field[None] + jnp.einsum(
        "mou,ut->mto", hidden_embedding, decoder_matrix, preferred_element_type=F32
    )
    groups = lax.axis_size(MEMBER)
    span = nodes // groups
    channels = forecast.shape[1]
    offset = lax.axis_index(MEMBER) * span
    by_node = forecast.reshape(members, channels, groups, span).transpose(2, 1, 0, 3)
    everyone = lax.all_to_all(
        by_node.reshape(groups, channels, members * span), MEMBER, 0, 0, tiled=True
    )
    observed = lax.dynamic_slice_in_dim(truth_field, offset, span, 1)
    area = lax.dynamic_slice_in_dim(cell_surface_share, offset, span, 0)
    derivative = score_gradient(
        everyone, jnp.tile(observed, (1, members)), jnp.tile(area[None], (1, members))
    )
    returned = lax.all_to_all(derivative, MEMBER, 0, 0, tiled=True)
    returned, *near = lax.optimization_barrier((returned, *near))
    x_after, x_before, z_after, z_before = near
    x_far, z_far = ring_far(x_after, x_before, "x"), ring_far(z_after, z_before, "z")
    grad_forecast = (
        returned.reshape(groups, channels, members, span)
        .transpose(2, 1, 0, 3)
        .reshape(members, channels, nodes)
    )

    shard_ids = jnp.arange(SIDE * SIDE, dtype=jnp.int32)
    around = jnp.arange(SIDE, dtype=jnp.int32)
    named = jnp.sum(
        jnp.where(kv_owner[:, :, None] == shard_ids[None, None, :], kv_local[:, :, None], 0), axis=1
    ).reshape(SIDE, SIDE, SIDE, SIDE)
    x_near = ((x_at + around) % SIDE)[:, None] == around[None, :]
    z_near = ((z_at + around) % SIDE)[:, None] == around[None, :]
    x_here, z_here = x_near[0], z_near[0]

    def picked(sx, sz, ox, oz):
        chosen = (
            sx[:, None, None, None, :, None, None, None]
            & sz[None, :, None, None, None, :, None, None]
            & ox[None, None, :, None, None, None, :, None]
            & oz[None, None, None, :, None, None, None, :]
        )
        return jnp.sum(jnp.where(chosen, named, 0), axis=(4, 5, 6, 7)).reshape(-1)

    tables = jnp.stack(
        [
            picked(x_here[None], z_near, x_near, z_here[None]),
            picked(x_near, z_here[None], x_here[None], z_near),
            jnp.pad((x_at + around) % SIDE, (0, SIDE * (SIDE - 1))),
        ]
    )

    permuter = (node_order[0][:, None] == jnp.arange(nodes, dtype=jnp.int32)[None, :]).astype(BF16)
    grad_columns = jnp.einsum(
        "mcg,tg->mct", grad_forecast, permuter, preferred_element_type=F32
    ).astype(BF16)
    grad_latent = jnp.einsum(
        "wc,mct->mwt", decoder_matrix, grad_columns, preferred_element_type=F32
    ).astype(BF16)
    saved = jnp.einsum("mgw,tg->mwt", hidden_embedding, permuter, preferred_element_type=F32).astype(
        BF16
    )
    split = (members, heads, width // heads, nodes)
    delta = jnp.sum(
        grad_latent.astype(F32).reshape(split) * saved.astype(F32).reshape(split), axis=2
    )
    late_own = jnp.concatenate(
        [grad_columns] + [part[n] for n in range(2) for part in (two_parts(row_lse), two_parts(delta))],
        axis=1,
    )
    late_z = [fetched(late_own[0], "z", d) for d in (1, 2, 3)]
    late_x = [fetched(late_own[1], "x", d) for d in (1, 2, 3)]

    outs = None
    parts = []
    for half in range(2):
        send_x, own, send_z = attention_tiles(
            half,
            tables,
            key_rows,
            value_rows,
            query,
            (x_after, x_far[half], x_before),
            (z_after, z_far[half], z_before),
            late_own,
            late_x,
            late_z,
            decoder_matrix,
        )
        if parts:
            (first_x, first_own, first_z) = parts[0]
            send_x, send_z, first_x, first_z = lax.optimization_barrier(
                (send_x, send_z, first_x, first_z)
            )
            parts[0] = (first_x, first_own, first_z)
        got_x = lax.all_to_all(send_x, "x", 0, 0, tiled=True)
        got_z = [delivered(send_z[d - 1], "z", d) for d in (1, 2, 3)]
        parts.append((got_x, own, got_z))
    for half, part in enumerate(parts):
        outs = summed(half, *part, outs)
    grad_key, grad_value, grad_query = outs
    return grad_query, grad_key, grad_value


def solution(mesh):
    finer = Mesh(mesh.devices.reshape(4, 2, SIDE, SIDE), ("y", "core", "x", "z"))
    plane = ("x", "z")
    in_specs = (
        P(MEMBER, plane, None),
        P(),
        P(None, plane),
        P(None, plane),
        P(plane),
        P(plane, None),
        P(MEMBER, plane, None),
        P(MEMBER, plane, None),
        P(MEMBER, plane, None),
        P(MEMBER, None, plane),
        P(),
        P(),
    )
    out_specs = (P(MEMBER, plane, None), P(MEMBER, plane, None), P(MEMBER, plane, None))
    return jax.shard_map(
        shards, mesh=finer, in_specs=in_specs, out_specs=out_specs, check_vma=False
    )
```

```python
import functools
import math

import jax
import jax.numpy as jnp
from jax import lax
from jax.experimental import pallas as pl
from jax.experimental.pallas import tpu as pltpu
from jax.sharding import Mesh
from jax.sharding import PartitionSpec as P

KB = 128
SIDE = 4
MEMBER = ("y", "core")
LOSS_SCALE = 4096.0
FAIR_EPS = 0.05
NORM_EPS = 1e-06
LOG2E = math.log2(math.e)
F32 = jnp.float32
BF16 = jnp.bfloat16


def score_kernel(forecast_ref, truth_ref, area_ref, out_ref):
    groups, _, lanes = forecast_ref.shape
    count = 2 * groups
    swapped = [pltpu.roll(forecast_ref[j], lanes // 2, 1) for j in range(groups)]

    def unit(x):
        return x * (1.0 / jnp.sqrt(jnp.sum(x * x, axis=0, keepdims=True) + NORM_EPS))

    weight = LOSS_SCALE * area_ref[...]
    for j in range(groups):
        one = forecast_ref[j]
        total = unit(one - swapped[j])
        for k in range(groups):
            if k != j:
                total = total + unit(one - forecast_ref[k]) + unit(one - swapped[k])
        gradient = weight * (
            unit(one - truth_ref[...]) / count - (1.0 - FAIR_EPS) / (count * (count - 1)) * total
        )
        out_ref[j] = gradient.astype(BF16)


def score_gradient(forecasts, truth, area):
    return pl.pallas_call(
        score_kernel, out_shape=jax.ShapeDtypeStruct(forecasts.shape, BF16), name="score_gradient"
    )(forecasts, truth, area)


def two_parts(x):
    high = x.astype(BF16)
    return [high, (x - lax.reduce_precision(x, 8, 7)).astype(BF16)]


def fetched(x, axis, distance):
    return lax.ppermute(x, axis, [(i, (i - distance) % SIDE) for i in range(SIDE)])


def delivered(x, axis, distance):
    return lax.ppermute(x, axis, [(i, (i + distance) % SIDE) for i in range(SIDE)])


def head_pair_tiles(table, base, kv, queries, lates, decoder, out, scratch):
    q_stack, g_stack, stat_rows, joined, dk_acc, dv_acc, dq_acc = scratch
    rows = q_stack.shape[1] // 2
    channels = decoder.shape[1]
    head = pl.program_id(0) * 2 + base
    head_dim = 64
    score_scale = head_dim ** (-0.5)
    lane = lax.broadcasted_iota(jnp.int32, (rows, 2 * head_dim), 1)
    first = lane < head_dim
    nt = (((1,), (1,)), ((), ()))
    tn = (((0,), (1,)), ((), ()))
    for t in range(SIDE):
        q = queries[t][...].astype(F32)
        g = lax.dot_general(
            lates[t][:channels, :], decoder[...], tn, preferred_element_type=F32
        )
        q_stack[t, :rows] = jnp.where(first, q, 0.0).astype(BF16)
        q_stack[t, rows:] = jnp.where(first, 0.0, q).astype(BF16)
        g_stack[t, :rows] = jnp.where(first, g, 0.0).astype(BF16)
        g_stack[t, rows:] = jnp.where(first, 0.0, g).astype(BF16)
        stat = lates[t][channels:, :].astype(F32)
        joined[: stat.shape[0] // 2] = stat[: stat.shape[0] // 2] + stat[stat.shape[0] // 2 :]
        for n in range(2):
            stat_rows[t, n : n + 1, :rows] = joined[pl.ds(8 * n + head, 1), :]
            stat_rows[t, n : n + 1, rows:] = joined[pl.ds(8 * n + head + 1, 1), :]
    dk_acc[...] = jnp.zeros_like(dk_acc)
    dv_acc[...] = jnp.zeros_like(dv_acc)

    def one_query_block(t, carry):
        q = q_stack[t]
        g = g_stack[t]
        lse = stat_rows[t, 0:1, :] * LOG2E
        delta = stat_rows[t, 1:2, :]
        dq_acc[...] = jnp.zeros_like(dq_acc)
        for pair in ((0, 1), (2, 3)):
            starts = [pl.multiple_of(table[t * SIDE + a] * KB, KB) for a in pair]
            k = jnp.concatenate([kv[a][0][pl.ds(s, KB), :] for a, s in zip(pair, starts)], axis=0)
            v = jnp.concatenate([kv[a][1][pl.ds(s, KB), :] for a, s in zip(pair, starts)], axis=0)
            scores = lax.dot_general(k, q, nt, preferred_element_type=F32)
            p = jnp.exp2(scores * (score_scale * LOG2E) - lse)
            dp = lax.dot_general(v, g, nt, preferred_element_type=F32)
            ds = (p * (dp - delta)).astype(BF16)
            dv = jnp.dot(p.astype(BF16), g, preferred_element_type=F32)
            dk = jnp.dot(ds, q, preferred_element_type=F32)
            for n, (a, s) in enumerate(zip(pair, starts)):
                dv_acc[a, pl.ds(s, KB), :] += dv[n * KB : (n + 1) * KB]
                dk_acc[a, pl.ds(s, KB), :] += dk[n * KB : (n + 1) * KB]
            kt = k.T
            dq_acc[:head_dim] += jnp.dot(kt[:head_dim], ds[:, :rows], preferred_element_type=F32)
            dq_acc[head_dim:] += jnp.dot(kt[head_dim:], ds[:, rows:], preferred_element_type=F32)
        dq = dq_acc[...].T * score_scale
        for n in range(SIDE):

            @pl.when(t == n)
            def _():
                out(2, n, dq)

        return carry

    lax.fori_loop(0, SIDE, one_query_block, 0)
    for a in range(SIDE):
        out(0, a, dk_acc[a] * score_scale)
        out(1, a, dv_acc[a])


def tile_kernel(table, *refs, base):
    key_own, value_own, query_own, late_own, decoder = refs[0:5]
    fetch_x, fetch_z = refs[5:8], refs[8:11]
    late_x, late_z = refs[11:14], refs[14:17]
    send_x, own_z, send_z = refs[17], refs[18], refs[19:22]
    scratch = refs[22:]
    sides = ((fetch_x, late_x), (fetch_z, late_z))
    for m in range(2):
        key_fetch = sides[m][0]
        query_fetch, late = sides[1 - m]
        kv = [(key_own.at[m], value_own.at[m])] + [(r.at[0], r.at[1]) for r in key_fetch]
        queries = [query_own.at[m]] + [r.at[2] for r in query_fetch]
        lates = [late_own.at[m]] + list(late)

        def out(kind, n, value, m=m):
            if m == (1 if kind == 2 else 0):
                send_x[table[2, n], kind] = value.astype(BF16)
            elif n == 0:
                own_z[kind] = value
            else:
                send_z[n - 1][kind] = value.astype(BF16)

        head_pair_tiles(
            table.at[m], base, kv, queries, lates, decoder, out, scratch
        )


def attention_tiles(half, tables, key_rows, value_rows, query, fetched_x, fetched_z, late_own, late_x, late_z, decoder_matrix):
    members, rows, width = key_rows.shape
    stats, channels = late_own.shape[1], decoder_matrix.shape[1]
    pairs = width // 256
    base = half * pairs
    own_spec = pl.BlockSpec((members, rows, 128), lambda h, tab: (0, 0, base + h))
    far_spec = pl.BlockSpec((3, rows, 128), lambda h, tab: (0, 0, h))
    late_spec = pl.BlockSpec((stats, rows), lambda h, tab: (0, 0))
    out = pl.pallas_call(
        functools.partial(tile_kernel, base=2 * base),
        out_shape=[
            jax.ShapeDtypeStruct((SIDE, 3, rows, width // 2), BF16),
            jax.ShapeDtypeStruct((3, rows, width // 2), F32),
        ]
        + [jax.ShapeDtypeStruct((3, rows, width // 2), BF16)] * 3,
        grid_spec=pltpu.PrefetchScalarGridSpec(
            num_scalar_prefetch=1,
            grid=(pairs,),
            in_specs=[own_spec] * 3
            + [
                pl.BlockSpec((members, stats, rows), lambda h, tab: (0, 0, 0)),
                pl.BlockSpec((128, channels), lambda h, tab: (base + h, 0)),
            ]
            + [far_spec] * 6
            + [late_spec] * 6,
            out_specs=[pl.BlockSpec((SIDE, 3, rows, 128), lambda h, tab: (0, 0, 0, h))]
            + [far_spec] * 4,
            scratch_shapes=[
                pltpu.VMEM((SIDE, 2 * rows, 128), BF16),
                pltpu.VMEM((SIDE, 2 * rows, 128), BF16),
                pltpu.VMEM((SIDE, 2, 2 * rows), F32),
                pltpu.VMEM((16, rows), F32),
                pltpu.VMEM((SIDE, rows, 128), F32),
                pltpu.VMEM((SIDE, rows, 128), F32),
                pltpu.VMEM((128, rows), F32),
            ],
        ),
        compiler_params=pltpu.CompilerParams(
            dimension_semantics=("arbitrary",), vmem_limit_bytes=50 * 1024 * 1024
        ),
        cost_estimate=pl.CostEstimate(
            flops=5 * 2 * (SIDE * SIDE * KB) * rows * 128 * 4 * pairs * members,
            transcendentals=SIDE * SIDE * KB * rows * 2 * pairs * members,
            bytes_accessed=20 * 1024 * 1024,
        ),
        name="attention_tiles",
    )(
        tables,
        *in_hbm(key_rows, value_rows, query, late_own, decoder_matrix),
        *in_hbm(*fetched_x, *fetched_z, *late_x, *late_z),
    )
    return out[0], out[1], out[2:]


def sum_kernel(got_x, own_z, *refs):
    got_z, outs = refs[:3], refs[-3:]
    for kind, ref in enumerate(outs):
        along_x = got_x[0, kind].astype(F32)
        for n in range(1, SIDE):
            along_x = along_x + got_x[n, kind].astype(F32)
        along_z = own_z[kind]
        for got in got_z:
            along_z = along_z + got[kind].astype(F32)
        ref[1 if kind == 2 else 0] = along_x
        ref[0 if kind == 2 else 1] = along_z


def summed(half, got_x, own_z, got_z, outs):
    _, rows, lanes = own_z.shape
    z_spec = pl.BlockSpec((3, rows // 2, lanes), lambda r: (0, r, 0))
    shape = jax.ShapeDtypeStruct((2, rows, 2 * lanes), F32)
    kept = list(outs) if outs else []
    return pl.pallas_call(
        sum_kernel,
        out_shape=[shape] * 3,
        grid=(2,),
        in_specs=[pl.BlockSpec((SIDE, 3, rows // 2, lanes), lambda r: (0, 0, r, 0))]
        + [z_spec] * 4
        + [pl.BlockSpec(memory_space=pl.ANY)] * len(kept),
        out_specs=[pl.BlockSpec((2, rows // 2, lanes), lambda r: (0, r, half))] * 3,
        input_output_aliases={5 + n: n for n in range(len(kept))},
        compiler_params=pltpu.CompilerParams(vmem_limit_bytes=50 * 1024 * 1024),
        name="summed",
    )(*in_hbm(got_x, own_z, *got_z), *kept)


def outgoing(half, *arrays):
    lanes = arrays[0].shape[-1] // 2
    return jnp.stack([a[:, half * lanes : (half + 1) * lanes] for a in arrays])


def in_hbm(*arrays):
    return [pltpu.with_memory_space_constraint(a, pltpu.HBM) for a in arrays]


def shards(
    hidden_embedding,
    decoder_matrix,
    baseline_field,
    truth_field,
    cell_surface_share,
    node_order,
    query,
    key_rows,
    value_rows,
    row_lse,
    kv_owner,
    kv_local,
):
    members, nodes, width = hidden_embedding.shape
    heads = row_lse.shape[1]
    x_at = lax.axis_index("x")
    z_at = lax.axis_index("z")

    own = [
        (outgoing(h, key_rows[0], value_rows[0], query[1]), outgoing(h, key_rows[1], value_rows[1], query[0]))
        for h in range(2)
    ]
    near = [fetched(a, axis, d) for a, axis in zip(own[0], ("x", "z")) for d in (1, 3)]

    forecast = baseline_field[None] + jnp.einsum(
        "mou,ut->mto", hidden_embedding, decoder_matrix, preferred_element_type=F32
    )
    groups = lax.axis_size(MEMBER)
    span = nodes // groups
    channels = forecast.shape[1]
    offset = lax.axis_index(MEMBER) * span
    by_node = forecast.reshape(members, channels, groups, span).transpose(2, 1, 0, 3)
    everyone = lax.all_to_all(
        by_node.reshape(groups, channels, members * span), MEMBER, 0, 0, tiled=True
    )
    observed = lax.dynamic_slice_in_dim(truth_field, offset, span, 1)
    area = lax.dynamic_slice_in_dim(cell_surface_share, offset, span, 0)
    derivative = score_gradient(
        everyone, jnp.tile(observed, (1, members)), jnp.tile(area[None], (1, members))
    )
    derivative, own_1, near = lax.optimization_barrier((derivative, own[1], near))
    returned = lax.all_to_all(derivative, MEMBER, 0, 0, tiled=True)
    far = [fetched(near[0], "x", 1), fetched(near[2], "z", 1)]
    before = [fetched(a, axis, 3) for a, axis in zip(own_1, ("x", "z"))]
    returned, own_1, before = lax.optimization_barrier((returned, own_1, before))
    grad_forecast = (
        returned.reshape(groups, channels, members, span)
        .transpose(2, 1, 0, 3)
        .reshape(members, channels, nodes)
    )

    shard_ids = jnp.arange(SIDE * SIDE, dtype=jnp.int32)
    around = jnp.arange(SIDE, dtype=jnp.int32)
    named = jnp.sum(
        jnp.where(kv_owner[:, :, None] == shard_ids[None, None, :], kv_local[:, :, None], 0), axis=1
    ).reshape(SIDE, SIDE, SIDE, SIDE)
    x_near = ((x_at + around) % SIDE)[:, None] == around[None, :]
    z_near = ((z_at + around) % SIDE)[:, None] == around[None, :]
    x_here, z_here = x_near[0], z_near[0]

    def picked(sx, sz, ox, oz):
        chosen = (
            sx[:, None, None, None, :, None, None, None]
            & sz[None, :, None, None, None, :, None, None]
            & ox[None, None, :, None, None, None, :, None]
            & oz[None, None, None, :, None, None, None, :]
        )
        return jnp.sum(jnp.where(chosen, named, 0), axis=(4, 5, 6, 7)).reshape(-1)

    tables = jnp.stack(
        [
            picked(x_here[None], z_near, x_near, z_here[None]),
            picked(x_near, z_here[None], x_here[None], z_near),
            jnp.pad((x_at + around) % SIDE, (0, SIDE * (SIDE - 1))),
        ]
    )

    permuter = (node_order[0][:, None] == jnp.arange(nodes, dtype=jnp.int32)[None, :]).astype(BF16)
    grad_columns = jnp.einsum(
        "mcg,tg->mct", grad_forecast, permuter, preferred_element_type=F32
    ).astype(BF16)
    grad_latent = jnp.einsum(
        "wc,mct->mwt", decoder_matrix, grad_columns, preferred_element_type=F32
    ).astype(BF16)
    saved = jnp.einsum("mgw,tg->mwt", hidden_embedding, permuter, preferred_element_type=F32).astype(
        BF16
    )
    split = (members, heads, width // heads, nodes)
    delta = jnp.sum(
        grad_latent.astype(F32).reshape(split) * saved.astype(F32).reshape(split), axis=2
    )
    late_own = jnp.concatenate(
        [grad_columns] + [part[n] for n in range(2) for part in (two_parts(row_lse), two_parts(delta))],
        axis=1,
    )
    late_z = [fetched(late_own[0], "z", d) for d in (1, 2, 3)]
    late_x = [fetched(late_own[1], "x", d) for d in (1, 2, 3)]
    late_own, own_1, before = lax.optimization_barrier((late_own, own_1, before))
    after = [fetched(a, axis, 1) for a, axis in zip(own_1, ("x", "z"))]
    last = [fetched(before[0], "x", 3), fetched(before[1], "z", 3)]
    came = (
        ((near[0], far[0], near[1]), (near[2], far[1], near[3])),
        ((after[0], last[0], before[0]), (after[1], last[1], before[1])),
    )

    outs = None
    parts = []
    for half in range(2):
        send_x, own, send_z = attention_tiles(
            half,
            tables,
            key_rows,
            value_rows,
            query,
            *came[half],
            late_own,
            late_x,
            late_z,
            decoder_matrix,
        )
        if parts:
            (first_x, first_own, first_z) = parts[0]
            send_x, send_z, first_x, first_z = lax.optimization_barrier(
                (send_x, send_z, first_x, first_z)
            )
            parts[0] = (first_x, first_own, first_z)
        got_x = lax.all_to_all(send_x, "x", 0, 0, tiled=True)
        got_z = [delivered(send_z[d - 1], "z", d) for d in (1, 2, 3)]
        parts.append((got_x, own, got_z))
    for half, part in enumerate(parts):
        outs = summed(half, *part, outs)
    grad_key, grad_value, grad_query = outs
    return grad_query, grad_key, grad_value


def solution(mesh):
    finer = Mesh(mesh.devices.reshape(4, 2, SIDE, SIDE), ("y", "core", "x", "z"))
    plane = ("x", "z")
    in_specs = (
        P(MEMBER, plane, None),
        P(),
        P(None, plane),
        P(None, plane),
        P(plane),
        P(plane, None),
        P(MEMBER, plane, None),
        P(MEMBER, plane, None),
        P(MEMBER, plane, None),
        P(MEMBER, None, plane),
        P(),
        P(),
    )
    out_specs = (P(MEMBER, plane, None), P(MEMBER, plane, None), P(MEMBER, plane, None))
    return jax.shard_map(
        shards, mesh=finer, in_specs=in_specs, out_specs=out_specs, check_vma=False
    )
```

```python
import functools
import math

import jax
import jax.numpy as jnp
from jax import lax
from jax.experimental import pallas as pl
from jax.experimental.pallas import tpu as pltpu
from jax.sharding import Mesh
from jax.sharding import PartitionSpec as P

KB = 128
SIDE = 4
GROUP = 2
MEMBER = ("y", "core")
LOSS_SCALE = 4096.0
FAIR_EPS = 0.05
NORM_EPS = 1e-06
LOG2E = math.log2(math.e)
F32 = jnp.float32
BF16 = jnp.bfloat16


def score_kernel(forecast_ref, truth_ref, area_ref, out_ref, swapped_ref):
    groups, _, lanes = forecast_ref.shape
    count = 2 * groups
    for k in range(groups):
        swapped_ref[k] = pltpu.roll(forecast_ref[k], lanes // 2, 1)
    weight = LOSS_SCALE * area_ref[...]

    def unit(x):
        return x * (1.0 / jnp.sqrt(jnp.sum(x * x, axis=0, keepdims=True) + NORM_EPS))

    def one_group(j, carry):
        one = forecast_ref[j]
        total = jnp.zeros_like(one)
        for k in range(groups):
            total = total + unit(one - forecast_ref[k]) + unit(one - swapped_ref[k])
        gradient = weight * (
            unit(one - truth_ref[...]) / count - (1.0 - FAIR_EPS) / (count * (count - 1)) * total
        )
        out_ref[j] = gradient.astype(BF16)
        return carry

    lax.fori_loop(0, groups, one_group, 0)


def score_gradient(forecasts, truth, area):
    return pl.pallas_call(
        score_kernel,
        out_shape=jax.ShapeDtypeStruct(forecasts.shape, BF16),
        scratch_shapes=[pltpu.VMEM(forecasts.shape, F32)],
        name="score_gradient",
    )(forecasts, truth, area)


def two_parts(x):
    high = x.astype(BF16)
    return [high, (x - lax.reduce_precision(x, 8, 7)).astype(BF16)]


def fetched(x, axis, distance):
    return lax.ppermute(x, axis, [(i, (i - distance) % SIDE) for i in range(SIDE)])


def delivered(x, axis, distance):
    return lax.ppermute(x, axis, [(i, (i + distance) % SIDE) for i in range(SIDE)])


def head_pair_tiles(table, scratch):
    kv_rows, q_rows, g_rows, lse_rows, delta_rows, dq_rows, dk_acc, dv_acc = scratch
    head_dim = 64
    score_scale = head_dim ** (-0.5)
    keys = GROUP * KB
    first = lax.broadcasted_iota(jnp.int32, (keys, 2 * head_dim), 1) < head_dim
    nt = (((1,), (1,)), ((), ()))
    dk_acc[...] = jnp.zeros_like(dk_acc)
    dv_acc[...] = jnp.zeros_like(dv_acc)

    def by_head(x):
        x = x.astype(F32)
        return jnp.concatenate(
            [jnp.where(first, x, 0.0).astype(BF16), jnp.where(first, 0.0, x).astype(BF16)], axis=0
        )

    for t in range(SIDE):
        q, g = q_rows[t], g_rows[t]
        dq = None
        for start in range(0, SIDE, GROUP):
            group = range(start, start + GROUP)
            starts = [pl.multiple_of(table[t * SIDE + a] * KB, KB) for a in group]
            k, v = (
                by_head(
                    jnp.concatenate([kv_rows[a, i, pl.ds(s, KB), :] for a, s in zip(group, starts)], axis=0)
                )
                for i in range(2)
            )
            scores = lax.dot_general(k, q, nt, preferred_element_type=F32)
            dp = lax.dot_general(v, g, nt, preferred_element_type=F32)
            ps, dss = [], []
            for n in range(2):
                part = slice(n * keys, (n + 1) * keys)
                p = jnp.exp2(scores[part] * (score_scale * LOG2E) - lse_rows[t, n : n + 1, :] * LOG2E)
                ps.append(p.astype(BF16))
                dss.append((p * (dp[part] - delta_rows[t, n : n + 1, :])).astype(BF16))
            p, ds = jnp.concatenate(ps, axis=0), jnp.concatenate(dss, axis=0)
            dv = jnp.dot(p, g, preferred_element_type=F32)
            dk = jnp.dot(ds, q, preferred_element_type=F32)
            dv = jnp.where(first, dv[:keys], dv[keys:])
            dk = jnp.where(first, dk[:keys], dk[keys:])
            for n, (a, s) in enumerate(zip(group, starts)):
                dv_acc[a, pl.ds(s, KB), :] += dv[n * KB : (n + 1) * KB]
                dk_acc[a, pl.ds(s, KB), :] += dk[n * KB : (n + 1) * KB]
            part = jnp.dot(k.T, ds, preferred_element_type=F32)
            dq = part if dq is None else dq + part
        dq_rows[t] = dq.T


def tile_kernel(table, *refs, base):
    key_own, value_own, query_own, late_own, decoder = refs[0:5]
    fetch_x, fetch_z = refs[5:8], refs[8:11]
    late_x, late_z = refs[11:14], refs[14:17]
    send_x, own_z, send_z = refs[17], refs[18], refs[19:22]
    scratch = refs[22:]
    kv_rows, q_rows, g_rows, lse_rows, delta_rows, dq_rows, dk_acc, dv_acc = scratch
    sides = ((fetch_x, late_x), (fetch_z, late_z))
    channels = decoder.shape[1]
    head = pl.program_id(0) * 2 + base
    score_scale = 64 ** (-0.5)
    tn = (((0,), (1,)), ((), ()))

    def load(m):
        key_fetch = sides[m][0]
        query_fetch, late = sides[1 - m]
        for n in range(SIDE):
            kv_rows[n, 0] = key_own[m] if n == 0 else key_fetch[n - 1][0]
            kv_rows[n, 1] = value_own[m] if n == 0 else key_fetch[n - 1][1]
            q_rows[n] = query_own[m] if n == 0 else query_fetch[n - 1][2]
            package = late_own.at[m] if n == 0 else late[n - 1]
            g_rows[n] = lax.dot_general(
                package[:channels, :], decoder[...], tn, preferred_element_type=F32
            ).astype(BF16)
            stat = package[channels:, :].astype(F32)
            stat = stat[: stat.shape[0] // 2] + stat[stat.shape[0] // 2 :]
            lse_rows[n], delta_rows[n] = stat[:8], stat[8:]
            for i in range(2):
                lse_rows[n, i : i + 1, :], delta_rows[n, i : i + 1, :] = (
                    lse_rows[n, pl.ds(head + i, 1), :],
                    delta_rows[n, pl.ds(head + i, 1), :],
                )

    def store(m):
        def out(kind, n, value):
            if m == (1 if kind == 2 else 0):
                send_x[table[2, n], kind] = value.astype(BF16)
            elif n == 0:
                own_z[kind] = value
            else:
                send_z[n - 1][kind] = value.astype(BF16)

        for n in range(SIDE):
            out(0, n, dk_acc[n] * score_scale)
            out(1, n, dv_acc[n])
            out(2, n, dq_rows[n] * score_scale)

    def one_member(m, carry):
        for n in range(2):
            pl.when(m == n)(functools.partial(load, n))
        head_pair_tiles(table.at[m], scratch)
        for n in range(2):
            pl.when(m == n)(functools.partial(store, n))
        return carry

    lax.fori_loop(0, 2, one_member, 0)


def attention_tiles(half, tables, key_rows, value_rows, query, fetched_x, fetched_z, late_own, late_x, late_z, decoder_matrix):
    members, rows, width = key_rows.shape
    stats, channels = late_own.shape[1], decoder_matrix.shape[1]
    pairs = width // 256
    base = half * pairs
    own_spec = pl.BlockSpec((members, rows, 128), lambda h, tab: (0, 0, base + h))
    far_spec = pl.BlockSpec((3, rows, 128), lambda h, tab: (0, 0, h))
    late_spec = pl.BlockSpec((stats, rows), lambda h, tab: (0, 0))
    out = pl.pallas_call(
        functools.partial(tile_kernel, base=2 * base),
        out_shape=[
            jax.ShapeDtypeStruct((SIDE, 3, rows, width // 2), BF16),
            jax.ShapeDtypeStruct((3, rows, width // 2), F32),
        ]
        + [jax.ShapeDtypeStruct((3, rows, width // 2), BF16)] * 3,
        grid_spec=pltpu.PrefetchScalarGridSpec(
            num_scalar_prefetch=1,
            grid=(pairs,),
            in_specs=[own_spec] * 3
            + [
                pl.BlockSpec((members, stats, rows), lambda h, tab: (0, 0, 0)),
                pl.BlockSpec((128, channels), lambda h, tab: (base + h, 0)),
            ]
            + [far_spec] * 6
            + [late_spec] * 6,
            out_specs=[pl.BlockSpec((SIDE, 3, rows, 128), lambda h, tab: (0, 0, 0, h))]
            + [far_spec] * 4,
            scratch_shapes=[
                pltpu.VMEM((SIDE, 2, rows, 128), BF16),
                pltpu.VMEM((SIDE, rows, 128), BF16),
                pltpu.VMEM((SIDE, rows, 128), BF16),
                pltpu.VMEM((SIDE, 8, rows), F32),
                pltpu.VMEM((SIDE, 8, rows), F32),
                pltpu.VMEM((SIDE, rows, 128), F32),
                pltpu.VMEM((SIDE, rows, 128), F32),
                pltpu.VMEM((SIDE, rows, 128), F32),
            ],
        ),
        compiler_params=pltpu.CompilerParams(
            dimension_semantics=("arbitrary",), vmem_limit_bytes=50 * 1024 * 1024
        ),
        cost_estimate=pl.CostEstimate(
            flops=5 * 2 * (SIDE * SIDE * KB) * rows * 128 * 4 * pairs * members,
            transcendentals=SIDE * SIDE * KB * rows * 2 * pairs * members,
            bytes_accessed=20 * 1024 * 1024,
        ),
        name="attention_tiles",
    )(
        tables,
        *in_hbm(key_rows, value_rows, query, late_own, decoder_matrix),
        *in_hbm(*fetched_x, *fetched_z, *late_x, *late_z),
    )
    return in_hbm(out[0])[0], out[1], in_hbm(*out[2:])


def sum_kernel(got_x, own_z, *refs):
    got_z, outs = refs[:3], refs[-3:]
    for kind, ref in enumerate(outs):
        along_x = got_x[0, kind].astype(F32)
        for n in range(1, SIDE):
            along_x = along_x + got_x[n, kind].astype(F32)
        along_z = own_z[kind]
        for got in got_z:
            along_z = along_z + got[kind].astype(F32)
        ref[1 if kind == 2 else 0] = along_x
        ref[0 if kind == 2 else 1] = along_z


def summed(half, got_x, own_z, got_z, outs):
    _, rows, lanes = own_z.shape
    z_spec = pl.BlockSpec((3, rows // 4, lanes), lambda r: (0, r, 0))
    shape = jax.ShapeDtypeStruct((2, rows, 2 * lanes), F32)
    kept = list(outs) if outs else []
    return pl.pallas_call(
        sum_kernel,
        out_shape=[shape] * 3,
        grid=(4,),
        in_specs=[pl.BlockSpec((SIDE, 3, rows // 4, lanes), lambda r: (0, 0, r, 0))]
        + [z_spec] * 4
        + [pl.BlockSpec(memory_space=pl.ANY)] * len(kept),
        out_specs=[pl.BlockSpec((2, rows // 4, lanes), lambda r: (0, r, half))] * 3,
        input_output_aliases={5 + n: n for n in range(len(kept))},
        compiler_params=pltpu.CompilerParams(vmem_limit_bytes=50 * 1024 * 1024),
        name="summed",
    )(*in_hbm(got_x), own_z, *in_hbm(*got_z), *kept)


def pack_kernel(key_rows, value_rows, query, along_x, along_z, sems, *, half):
    lanes = along_x.shape[-1]
    part = pl.ds(half * lanes, lanes)
    copies = []
    for m, out in enumerate((along_x, along_z)):
        for n, ref in enumerate((key_rows.at[m], value_rows.at[m], query.at[1 - m])):
            copies.append(pltpu.make_async_copy(ref.at[:, part], out.at[n], sems.at[m, n]))
    for copy in copies:
        copy.start()
    for copy in copies:
        copy.wait()


def outgoing(half, key_rows, value_rows, query):
    _, rows, width = key_rows.shape
    anywhere = pl.BlockSpec(memory_space=pl.ANY)
    return pl.pallas_call(
        functools.partial(pack_kernel, half=half),
        out_shape=[jax.ShapeDtypeStruct((3, rows, width // 2), BF16)] * 2,
        in_specs=[anywhere] * 3,
        out_specs=[anywhere] * 2,
        scratch_shapes=[pltpu.SemaphoreType.DMA((2, 3))],
        name="outgoing",
    )(*in_hbm(key_rows, value_rows, query))


def in_hbm(*arrays):
    return [pltpu.with_memory_space_constraint(a, pltpu.HBM) for a in arrays]


def shards(
    hidden_embedding,
    decoder_matrix,
    baseline_field,
    truth_field,
    cell_surface_share,
    node_order,
    query,
    key_rows,
    value_rows,
    row_lse,
    kv_owner,
    kv_local,
):
    members, nodes, width = hidden_embedding.shape
    heads = row_lse.shape[1]
    x_at = lax.axis_index("x")
    z_at = lax.axis_index("z")

    own_0 = outgoing(0, key_rows, value_rows, query)
    near = [fetched(a, axis, d) for a, axis in zip(own_0, ("x", "z")) for d in (1, 3)]
    own_1 = outgoing(1, key_rows, value_rows, query)

    forecast = baseline_field[None] + jnp.einsum(
        "mou,ut->mto", hidden_embedding, decoder_matrix, preferred_element_type=F32
    )
    groups = lax.axis_size(MEMBER)
    span = nodes // groups
    channels = forecast.shape[1]
    offset = lax.axis_index(MEMBER) * span
    by_node = forecast.reshape(members, channels, groups, span).transpose(2, 1, 0, 3)
    everyone = lax.all_to_all(
        by_node.reshape(groups, channels, members * span), MEMBER, 0, 0, tiled=True
    )
    observed = lax.dynamic_slice_in_dim(truth_field, offset, span, 1)
    area = lax.dynamic_slice_in_dim(cell_surface_share, offset, span, 0)
    derivative = score_gradient(
        everyone, jnp.tile(observed, (1, members)), jnp.tile(area[None], (1, members))
    )
    derivative, own_1, near, decoder_rows = lax.optimization_barrier(
        (derivative, own_1, near, in_hbm(decoder_matrix)[0])
    )
    returned = lax.all_to_all(derivative, MEMBER, 0, 0, tiled=True)
    far = [fetched(near[0], "x", 1), fetched(near[2], "z", 1)]
    before = [fetched(a, axis, 3) for a, axis in zip(own_1, ("x", "z"))]
    grad_forecast = (
        returned.reshape(groups, channels, members, span)
        .transpose(2, 1, 0, 3)
        .reshape(members, channels, nodes)
    )

    shard_ids = jnp.arange(SIDE * SIDE, dtype=jnp.int32)
    around = jnp.arange(SIDE, dtype=jnp.int32)
    named = jnp.sum(
        jnp.where(kv_owner[:, :, None] == shard_ids[None, None, :], kv_local[:, :, None], 0), axis=1
    ).reshape(SIDE, SIDE, SIDE, SIDE)
    x_near = ((x_at + around) % SIDE)[:, None] == around[None, :]
    z_near = ((z_at + around) % SIDE)[:, None] == around[None, :]
    x_here, z_here = x_near[0], z_near[0]

    def picked(sx, sz, ox, oz):
        chosen = (
            sx[:, None, None, None, :, None, None, None]
            & sz[None, :, None, None, None, :, None, None]
            & ox[None, None, :, None, None, None, :, None]
            & oz[None, None, None, :, None, None, None, :]
        )
        return jnp.sum(jnp.where(chosen, named, 0), axis=(4, 5, 6, 7)).reshape(-1)

    tables = jnp.stack(
        [
            picked(x_here[None], z_near, x_near, z_here[None]),
            picked(x_near, z_here[None], x_here[None], z_near),
            jnp.pad((x_at + around) % SIDE, (0, SIDE * (SIDE - 1))),
        ]
    )

    permuter = (node_order[0][:, None] == jnp.arange(nodes, dtype=jnp.int32)[None, :]).astype(BF16)
    grad_columns = jnp.einsum(
        "mcg,tg->mct", grad_forecast, permuter, preferred_element_type=F32
    ).astype(BF16)
    grad_latent = jnp.einsum(
        "wc,mct->mwt", decoder_matrix, grad_columns, preferred_element_type=F32
    ).astype(BF16)
    saved = jnp.einsum("mgw,tg->mwt", hidden_embedding, permuter, preferred_element_type=F32).astype(
        BF16
    )
    split = (members, heads, width // heads, nodes)
    delta = jnp.sum(
        grad_latent.astype(F32).reshape(split) * saved.astype(F32).reshape(split), axis=2
    )
    late_own = jnp.concatenate(
        [grad_columns] + [part[n] for n in range(2) for part in (two_parts(row_lse), two_parts(delta))],
        axis=1,
    )
    late_z = [fetched(late_own[0], "z", d) for d in (1, 2, 3)]
    late_x = [fetched(late_own[1], "x", d) for d in (1, 2, 3)]
    late_own, own_1, before = lax.optimization_barrier((late_own, own_1, before))
    after = [fetched(a, axis, 1) for a, axis in zip(own_1, ("x", "z"))]
    last = [fetched(before[0], "x", 3), fetched(before[1], "z", 3)]
    came = (
        ((near[0], far[0], near[1]), (near[2], far[1], near[3])),
        ((after[0], last[0], before[0]), (after[1], last[1], before[1])),
    )

    outs = None
    parts = []
    for half in range(2):
        send_x, own, send_z = attention_tiles(
            half,
            tables,
            key_rows,
            value_rows,
            query,
            *came[half],
            late_own,
            late_x,
            late_z,
            decoder_rows,
        )
        if parts:
            (first_x, first_own, first_z) = parts[0]
            send_x, send_z, first_x, first_z = lax.optimization_barrier(
                (send_x, send_z, first_x, first_z)
            )
            parts[0] = (first_x, first_own, first_z)
        got_x = lax.all_to_all(send_x, "x", 0, 0, tiled=True)
        got_z = [delivered(send_z[d - 1], "z", d) for d in (1, 2, 3)]
        parts.append((got_x, own, got_z))
    for half, part in enumerate(parts):
        outs = summed(half, *part, outs)
    grad_key, grad_value, grad_query = outs
    return grad_query, grad_key, grad_value


def solution(mesh):
    finer = Mesh(mesh.devices.reshape(4, 2, SIDE, SIDE), ("y", "core", "x", "z"))
    plane = ("x", "z")
    in_specs = (
        P(MEMBER, plane, None),
        P(),
        P(None, plane),
        P(None, plane),
        P(plane),
        P(plane, None),
        P(MEMBER, plane, None),
        P(MEMBER, plane, None),
        P(MEMBER, plane, None),
        P(MEMBER, None, plane),
        P(),
        P(),
    )
    out_specs = (P(MEMBER, plane, None), P(MEMBER, plane, None), P(MEMBER, plane, None))
    return jax.shard_map(
        shards, mesh=finer, in_specs=in_specs, out_specs=out_specs, check_vma=False
    )
```

```python
import functools
import math

import jax
import jax.numpy as jnp
from jax import lax
from jax.experimental import pallas as pl
from jax.experimental.pallas import tpu as pltpu
from jax.sharding import Mesh
from jax.sharding import PartitionSpec as P

KB = 128
SIDE = 4
GROUP = 2
MEMBER = ("y", "core")
LOSS_SCALE = 4096.0
FAIR_EPS = 0.05
NORM_EPS = 1e-06
LOG2E = math.log2(math.e)
F32 = jnp.float32
BF16 = jnp.bfloat16


def score_kernel(forecast_ref, truth_ref, area_ref, out_ref, swapped_ref):
    groups, _, lanes = forecast_ref.shape
    count = 2 * groups
    for k in range(groups):
        swapped_ref[k] = pltpu.roll(forecast_ref[k], lanes // 2, 1)
    weight = LOSS_SCALE * area_ref[...]

    def unit(x):
        return x * (1.0 / jnp.sqrt(jnp.sum(x * x, axis=0, keepdims=True) + NORM_EPS))

    def one_group(j, carry):
        one = forecast_ref[j]
        total = jnp.zeros_like(one)
        for k in range(groups):
            total = total + unit(one - forecast_ref[k]) + unit(one - swapped_ref[k])
        gradient = weight * (
            unit(one - truth_ref[...]) / count - (1.0 - FAIR_EPS) / (count * (count - 1)) * total
        )
        out_ref[j] = gradient.astype(BF16)
        return carry

    lax.fori_loop(0, groups, one_group, 0)


def score_gradient(forecasts, truth, area):
    return pl.pallas_call(
        score_kernel,
        out_shape=jax.ShapeDtypeStruct(forecasts.shape, BF16),
        in_specs=[pl.BlockSpec(memory_space=pltpu.VMEM)] * 3,
        out_specs=pl.BlockSpec(memory_space=pltpu.VMEM),
        scratch_shapes=[pltpu.VMEM(forecasts.shape, F32)],
        name="score_gradient",
    )(forecasts, truth, area)


def two_parts(x):
    high = x.astype(BF16)
    return [high, (x - lax.reduce_precision(x, 8, 7)).astype(BF16)]


def fetched(x, axis, distance):
    return lax.ppermute(x, axis, [(i, (i - distance) % SIDE) for i in range(SIDE)])


def delivered(x, axis, distance):
    return lax.ppermute(x, axis, [(i, (i + distance) % SIDE) for i in range(SIDE)])


def head_pair_tiles(table, scratch):
    kv_rows, q_rows, g_rows, lse_rows, delta_rows, dq_rows, dk_acc, dv_acc = scratch
    head_dim = 64
    score_scale = head_dim ** (-0.5)
    keys = GROUP * KB
    first = lax.broadcasted_iota(jnp.int32, (keys, 2 * head_dim), 1) < head_dim
    nt = (((1,), (1,)), ((), ()))
    dk_acc[...] = jnp.zeros_like(dk_acc)
    dv_acc[...] = jnp.zeros_like(dv_acc)

    def by_head(x):
        x = x.astype(F32)
        return jnp.concatenate(
            [jnp.where(first, x, 0.0).astype(BF16), jnp.where(first, 0.0, x).astype(BF16)], axis=0
        )

    for t in range(SIDE):
        q, g = q_rows[t], g_rows[t]
        dq = None
        for start in range(0, SIDE, GROUP):
            group = range(start, start + GROUP)
            starts = [pl.multiple_of(table[t * SIDE + a] * KB, KB) for a in group]
            k, v = (
                by_head(
                    jnp.concatenate([kv_rows[a, i, pl.ds(s, KB), :] for a, s in zip(group, starts)], axis=0)
                )
                for i in range(2)
            )
            scores = lax.dot_general(k, q, nt, preferred_element_type=F32)
            dp = lax.dot_general(v, g, nt, preferred_element_type=F32)
            ps, dss = [], []
            for n in range(2):
                part = slice(n * keys, (n + 1) * keys)
                p = jnp.exp2(scores[part] * (score_scale * LOG2E) - lse_rows[t, n : n + 1, :] * LOG2E)
                ps.append(p.astype(BF16))
                dss.append((p * (dp[part] - delta_rows[t, n : n + 1, :])).astype(BF16))
            p, ds = jnp.concatenate(ps, axis=0), jnp.concatenate(dss, axis=0)
            dv = jnp.dot(p, g, preferred_element_type=F32)
            dk = jnp.dot(ds, q, preferred_element_type=F32)
            dv = jnp.where(first, dv[:keys], dv[keys:])
            dk = jnp.where(first, dk[:keys], dk[keys:])
            for n, (a, s) in enumerate(zip(group, starts)):
                dv_acc[a, pl.ds(s, KB), :] += dv[n * KB : (n + 1) * KB]
                dk_acc[a, pl.ds(s, KB), :] += dk[n * KB : (n + 1) * KB]
            part = jnp.dot(k.T, ds, preferred_element_type=F32)
            dq = part if dq is None else dq + part
        dq_rows[t] = dq.T


def tile_kernel(table, *refs, base):
    key_own, value_own, query_own, late_own, decoder = refs[0:5]
    fetch_x, fetch_z = refs[5:8], refs[8:11]
    late_x, late_z = refs[11:14], refs[14:17]
    send_x, own_z, send_z = refs[17], refs[18], refs[19:22]
    scratch = refs[22:]
    kv_rows, q_rows, g_rows, lse_rows, delta_rows, dq_rows, dk_acc, dv_acc = scratch
    sides = ((fetch_x, late_x), (fetch_z, late_z))
    channels = decoder.shape[1]
    head = pl.program_id(0) * 2 + base
    score_scale = 64 ** (-0.5)
    tn = (((0,), (1,)), ((), ()))

    def load(m):
        key_fetch = sides[m][0]
        query_fetch, late = sides[1 - m]
        for n in range(SIDE):
            kv_rows[n, 0] = key_own[m] if n == 0 else key_fetch[n - 1][0]
            kv_rows[n, 1] = value_own[m] if n == 0 else key_fetch[n - 1][1]
            q_rows[n] = query_own[m] if n == 0 else query_fetch[n - 1][2]
            package = late_own.at[m] if n == 0 else late[n - 1]
            g_rows[n] = lax.dot_general(
                package[:channels, :], decoder[...], tn, preferred_element_type=F32
            ).astype(BF16)
            stat = package[channels:, :].astype(F32)
            stat = stat[: stat.shape[0] // 2] + stat[stat.shape[0] // 2 :]
            lse_rows[n], delta_rows[n] = stat[:8], stat[8:]
            for i in range(2):
                lse_rows[n, i : i + 1, :], delta_rows[n, i : i + 1, :] = (
                    lse_rows[n, pl.ds(head + i, 1), :],
                    delta_rows[n, pl.ds(head + i, 1), :],
                )

    def store(m):
        def out(kind, n, value):
            if m == (1 if kind == 2 else 0):
                send_x[table[2, n], kind] = value.astype(BF16)
            elif n == 0:
                own_z[kind] = value
            else:
                send_z[n - 1][kind] = value.astype(BF16)

        for n in range(SIDE):
            out(0, n, dk_acc[n] * score_scale)
            out(1, n, dv_acc[n])
            out(2, n, dq_rows[n] * score_scale)

    def one_member(m, carry):
        for n in range(2):
            pl.when(m == n)(functools.partial(load, n))
        head_pair_tiles(table.at[m], scratch)
        for n in range(2):
            pl.when(m == n)(functools.partial(store, n))
        return carry

    lax.fori_loop(0, 2, one_member, 0)


def attention_tiles(half, tables, key_rows, value_rows, query, fetched_x, fetched_z, late_own, late_x, late_z, decoder_matrix):
    members, rows, width = key_rows.shape
    stats, channels = late_own.shape[1], decoder_matrix.shape[1]
    pairs = width // 256
    base = half * pairs
    own_spec = pl.BlockSpec((members, rows, 128), lambda h, tab: (0, 0, base + h))
    far_spec = pl.BlockSpec((3, rows, 128), lambda h, tab: (0, 0, h))
    late_spec = pl.BlockSpec((stats, rows), lambda h, tab: (0, 0))
    out = pl.pallas_call(
        functools.partial(tile_kernel, base=2 * base),
        out_shape=[
            pltpu.HBM((SIDE, 3, rows, width // 2), BF16),
            pltpu.HBM((3, rows, width // 2), F32),
        ]
        + [pltpu.HBM((3, rows, width // 2), BF16)] * 3,
        grid_spec=pltpu.PrefetchScalarGridSpec(
            num_scalar_prefetch=1,
            grid=(pairs,),
            in_specs=[own_spec] * 3
            + [
                pl.BlockSpec((members, stats, rows), lambda h, tab: (0, 0, 0)),
                pl.BlockSpec((128, channels), lambda h, tab: (base + h, 0)),
            ]
            + [far_spec] * 6
            + [late_spec] * 6,
            out_specs=[pl.BlockSpec((SIDE, 3, rows, 128), lambda h, tab: (0, 0, 0, h))]
            + [far_spec] * 4,
            scratch_shapes=[
                pltpu.VMEM((SIDE, 2, rows, 128), BF16),
                pltpu.VMEM((SIDE, rows, 128), BF16),
                pltpu.VMEM((SIDE, rows, 128), BF16),
                pltpu.VMEM((SIDE, 8, rows), F32),
                pltpu.VMEM((SIDE, 8, rows), F32),
                pltpu.VMEM((SIDE, rows, 128), F32),
                pltpu.VMEM((SIDE, rows, 128), F32),
                pltpu.VMEM((SIDE, rows, 128), F32),
            ],
        ),
        compiler_params=pltpu.CompilerParams(
            dimension_semantics=("arbitrary",), vmem_limit_bytes=50 * 1024 * 1024
        ),
        cost_estimate=pl.CostEstimate(
            flops=5 * 2 * (SIDE * SIDE * KB) * rows * 128 * 4 * pairs * members,
            transcendentals=SIDE * SIDE * KB * rows * 2 * pairs * members,
            bytes_accessed=20 * 1024 * 1024,
        ),
        name="attention_tiles",
    )(
        tables,
        *in_hbm(key_rows, value_rows, query, late_own, decoder_matrix),
        *in_hbm(*fetched_x, *fetched_z, *late_x, *late_z),
    )
    return out[0], out[1], out[2:]


def sum_kernel(got_x, own_z, *refs):
    got_z, outs = refs[:3], refs[-3:]
    for kind, ref in enumerate(outs):
        along_x = got_x[0, kind].astype(F32)
        for n in range(1, SIDE):
            along_x = along_x + got_x[n, kind].astype(F32)
        along_z = own_z[kind]
        for got in got_z:
            along_z = along_z + got[kind].astype(F32)
        ref[1 if kind == 2 else 0] = along_x
        ref[0 if kind == 2 else 1] = along_z


def summed(half, got_x, own_z, got_z, outs):
    _, rows, lanes = own_z.shape
    z_spec = pl.BlockSpec((3, rows // 2, lanes), lambda r: (0, r, 0))
    shape = jax.ShapeDtypeStruct((2, rows, 2 * lanes), F32)
    kept = list(outs) if outs else []
    return pl.pallas_call(
        sum_kernel,
        out_shape=[shape] * 3,
        grid=(2,),
        in_specs=[pl.BlockSpec((SIDE, 3, rows // 2, lanes), lambda r: (0, 0, r, 0))]
        + [z_spec] * 4
        + [pl.BlockSpec(memory_space=pl.ANY)] * len(kept),
        out_specs=[pl.BlockSpec((2, rows // 2, lanes), lambda r: (0, r, half))] * 3,
        input_output_aliases={5 + n: n for n in range(len(kept))},
        compiler_params=pltpu.CompilerParams(vmem_limit_bytes=50 * 1024 * 1024),
        name="summed",
    )(*in_hbm(got_x, own_z, *got_z), *kept)


def outgoing(half, key_rows, value_rows, query):
    lanes = query.shape[-1] // 2
    part = slice(half * lanes, (half + 1) * lanes)
    return [
        jnp.stack([key_rows[m, :, part], value_rows[m, :, part], query[1 - m, :, part]]) for m in range(2)
    ]


def in_hbm(*arrays):
    return [pltpu.with_memory_space_constraint(a, pltpu.HBM) for a in arrays]


def shards(
    hidden_embedding,
    decoder_matrix,
    baseline_field,
    truth_field,
    cell_surface_share,
    node_order,
    query,
    key_rows,
    value_rows,
    row_lse,
    kv_owner,
    kv_local,
):
    members, nodes, width = hidden_embedding.shape
    heads = row_lse.shape[1]
    x_at = lax.axis_index("x")
    z_at = lax.axis_index("z")

    own_0 = outgoing(0, key_rows, value_rows, query)
    near = [fetched(a, axis, d) for a, axis in zip(own_0, ("x", "z")) for d in (1, 3)]
    own_1 = outgoing(1, key_rows, value_rows, query)

    forecast = baseline_field[None] + jnp.einsum(
        "mou,ut->mto", hidden_embedding, decoder_matrix, preferred_element_type=F32
    )
    groups = lax.axis_size(MEMBER)
    span = nodes // groups
    channels = forecast.shape[1]
    offset = lax.axis_index(MEMBER) * span
    by_node = forecast.reshape(members, channels, groups, span).transpose(2, 1, 0, 3)
    everyone = lax.all_to_all(
        by_node.reshape(groups, channels, members * span), MEMBER, 0, 0, tiled=True
    )
    observed = lax.dynamic_slice_in_dim(truth_field, offset, span, 1)
    area = lax.dynamic_slice_in_dim(cell_surface_share, offset, span, 0)
    derivative = score_gradient(
        everyone, jnp.tile(observed, (1, members)), jnp.tile(area[None], (1, members))
    )
    derivative, own_1, near, decoder_rows = lax.optimization_barrier(
        (derivative, own_1, near, in_hbm(decoder_matrix)[0])
    )
    returned = lax.all_to_all(derivative, MEMBER, 0, 0, tiled=True)
    far = [fetched(near[0], "x", 1), fetched(near[2], "z", 1)]
    z_before = fetched(own_1[1], "z", 3)
    grad_forecast = (
        returned.reshape(groups, channels, members, span)
        .transpose(2, 1, 0, 3)
        .reshape(members, channels, nodes)
    )

    shard_ids = jnp.arange(SIDE * SIDE, dtype=jnp.int32)
    around = jnp.arange(SIDE, dtype=jnp.int32)
    named = jnp.sum(
        jnp.where(kv_owner[:, :, None] == shard_ids[None, None, :], kv_local[:, :, None], 0), axis=1
    ).reshape(SIDE, SIDE, SIDE, SIDE)
    x_near = ((x_at + around) % SIDE)[:, None] == around[None, :]
    z_near = ((z_at + around) % SIDE)[:, None] == around[None, :]
    x_here, z_here = x_near[0], z_near[0]

    def picked(sx, sz, ox, oz):
        chosen = (
            sx[:, None, None, None, :, None, None, None]
            & sz[None, :, None, None, None, :, None, None]
            & ox[None, None, :, None, None, None, :, None]
            & oz[None, None, None, :, None, None, None, :]
        )
        return jnp.sum(jnp.where(chosen, named, 0), axis=(4, 5, 6, 7)).reshape(-1)

    tables = jnp.stack(
        [
            picked(x_here[None], z_near, x_near, z_here[None]),
            picked(x_near, z_here[None], x_here[None], z_near),
            jnp.pad((x_at + around) % SIDE, (0, SIDE * (SIDE - 1))),
        ]
    )

    permuter = (node_order[0][:, None] == jnp.arange(nodes, dtype=jnp.int32)[None, :]).astype(BF16)
    grad_columns = jnp.einsum(
        "mcg,tg->mct", grad_forecast, permuter, preferred_element_type=F32
    ).astype(BF16)
    grad_latent = jnp.einsum(
        "wc,mct->mwt", decoder_matrix, grad_columns, preferred_element_type=F32
    ).astype(BF16)
    saved = jnp.einsum("mgw,tg->mwt", hidden_embedding, permuter, preferred_element_type=F32).astype(
        BF16
    )
    split = (members, heads, width // heads, nodes)
    delta = jnp.sum(
        grad_latent.astype(F32).reshape(split) * saved.astype(F32).reshape(split), axis=2
    )
    late_own = jnp.concatenate(
        [grad_columns] + [part[n] for n in range(2) for part in (two_parts(row_lse), two_parts(delta))],
        axis=1,
    )
    late_z = [fetched(late_own[0], "z", d) for d in (1, 2, 3)]
    late_x = [fetched(late_own[1], "x", d) for d in (1, 2, 3)]
    late_own, own_1, z_before = lax.optimization_barrier((late_own, own_1, z_before))
    x_around = [fetched(own_1[0], "x", d) for d in (1, 2, 3)]
    z_around = [fetched(own_1[1], "z", 1), fetched(z_before, "z", 3), z_before]
    came = (((near[0], far[0], near[1]), (near[2], far[1], near[3])), (x_around, z_around))

    outs = None
    parts = []
    for half in range(2):
        send_x, own, send_z = attention_tiles(
            half,
            tables,
            key_rows,
            value_rows,
            query,
            *came[half],
            late_own,
            late_x,
            late_z,
            decoder_rows,
        )
        if parts:
            (first_x, first_own, first_z) = parts[0]
            send_x, send_z, first_x, first_z = lax.optimization_barrier(
                (send_x, send_z, first_x, first_z)
            )
            parts[0] = (first_x, first_own, first_z)
        got_x = lax.all_to_all(send_x, "x", 0, 0, tiled=True)
        got_z = [delivered(send_z[d - 1], "z", d) for d in (1, 2, 3)]
        parts.append((got_x, own, got_z))
    for half, part in enumerate(parts):
        outs = summed(half, *part, outs)
    grad_key, grad_value, grad_query = outs
    return grad_query, grad_key, grad_value


def solution(mesh):
    finer = Mesh(mesh.devices.reshape(4, 2, SIDE, SIDE), ("y", "core", "x", "z"))
    plane = ("x", "z")
    in_specs = (
        P(MEMBER, plane, None),
        P(),
        P(None, plane),
        P(None, plane),
        P(plane),
        P(plane, None),
        P(MEMBER, plane, None),
        P(MEMBER, plane, None),
        P(MEMBER, plane, None),
        P(MEMBER, None, plane),
        P(),
        P(),
    )
    out_specs = (P(MEMBER, plane, None), P(MEMBER, plane, None), P(MEMBER, plane, None))
    return jax.shard_map(
        shards, mesh=finer, in_specs=in_specs, out_specs=out_specs, check_vma=False
    )
```

```python
import functools
import math

import jax
import jax.numpy as jnp
from jax import lax
from jax.experimental import pallas as pl
from jax.experimental.pallas import tpu as pltpu
from jax.sharding import Mesh
from jax.sharding import PartitionSpec as P

KB = 128
SIDE = 4
GROUP = 2
MEMBER = ("y", "core")
LOSS_SCALE = 4096.0
FAIR_EPS = 0.05
NORM_EPS = 1e-06
LOG2E = math.log2(math.e)
F32 = jnp.float32
BF16 = jnp.bfloat16


def score_kernel(forecast_ref, truth_ref, area_ref, out_ref, swapped_ref):
    groups, _, lanes = forecast_ref.shape
    count = 2 * groups
    for k in range(groups):
        swapped_ref[k] = pltpu.roll(forecast_ref[k], lanes // 2, 1)
    weight = LOSS_SCALE * area_ref[...]

    def unit(x):
        return x * (1.0 / jnp.sqrt(jnp.sum(x * x, axis=0, keepdims=True) + NORM_EPS))

    def one_group(j, carry):
        one = forecast_ref[j]
        total = jnp.zeros_like(one)
        for k in range(groups):
            total = total + unit(one - forecast_ref[k]) + unit(one - swapped_ref[k])
        gradient = weight * (
            unit(one - truth_ref[...]) / count - (1.0 - FAIR_EPS) / (count * (count - 1)) * total
        )
        out_ref[j] = gradient.astype(BF16)
        return carry

    lax.fori_loop(0, groups, one_group, 0)


def score_gradient(forecasts, truth, area):
    return pl.pallas_call(
        score_kernel,
        out_shape=jax.ShapeDtypeStruct(forecasts.shape, BF16),
        in_specs=[pl.BlockSpec(memory_space=pltpu.VMEM)] * 3,
        out_specs=pl.BlockSpec(memory_space=pltpu.VMEM),
        scratch_shapes=[pltpu.VMEM(forecasts.shape, F32)],
        name="score_gradient",
    )(forecasts, truth, area)


def two_parts(x):
    high = x.astype(BF16)
    return [high, (x - lax.reduce_precision(x, 8, 7)).astype(BF16)]


def fetched(x, axis, distance):
    return lax.ppermute(x, axis, [(i, (i - distance) % SIDE) for i in range(SIDE)])


def delivered(x, axis, distance):
    return lax.ppermute(x, axis, [(i, (i + distance) % SIDE) for i in range(SIDE)])


def head_pair_tiles(table, scratch):
    kv_rows, q_rows, g_rows, lse_rows, delta_rows, dq_rows, dk_acc, dv_acc = scratch
    head_dim = 64
    score_scale = head_dim ** (-0.5)
    keys = GROUP * KB
    first = lax.broadcasted_iota(jnp.int32, (keys, 2 * head_dim), 1) < head_dim
    nt = (((1,), (1,)), ((), ()))
    dk_acc[...] = jnp.zeros_like(dk_acc)
    dv_acc[...] = jnp.zeros_like(dv_acc)

    def by_head(x):
        x = x.astype(F32)
        return jnp.concatenate(
            [jnp.where(first, x, 0.0).astype(BF16), jnp.where(first, 0.0, x).astype(BF16)], axis=0
        )

    for t in range(SIDE):
        q, g = q_rows[t], g_rows[t]
        dq = None
        for start in range(0, SIDE, GROUP):
            group = range(start, start + GROUP)
            starts = [pl.multiple_of(table[t * SIDE + a] * KB, KB) for a in group]
            k, v = (
                by_head(
                    jnp.concatenate([kv_rows[a, i, pl.ds(s, KB), :] for a, s in zip(group, starts)], axis=0)
                )
                for i in range(2)
            )
            scores = lax.dot_general(k, q, nt, preferred_element_type=F32)
            dp = lax.dot_general(v, g, nt, preferred_element_type=F32)
            ps, dss = [], []
            for n in range(2):
                part = slice(n * keys, (n + 1) * keys)
                p = jnp.exp2(scores[part] * (score_scale * LOG2E) - lse_rows[t, n : n + 1, :] * LOG2E)
                ps.append(p.astype(BF16))
                dss.append((p * (dp[part] - delta_rows[t, n : n + 1, :])).astype(BF16))
            p, ds = jnp.concatenate(ps, axis=0), jnp.concatenate(dss, axis=0)
            dv = jnp.dot(p, g, preferred_element_type=F32)
            dk = jnp.dot(ds, q, preferred_element_type=F32)
            dv = jnp.where(first, dv[:keys], dv[keys:])
            dk = jnp.where(first, dk[:keys], dk[keys:])
            for n, (a, s) in enumerate(zip(group, starts)):
                dv_acc[a, pl.ds(s, KB), :] += dv[n * KB : (n + 1) * KB]
                dk_acc[a, pl.ds(s, KB), :] += dk[n * KB : (n + 1) * KB]
            part = jnp.dot(k.T, ds, preferred_element_type=F32)
            dq = part if dq is None else dq + part
        dq_rows[t] = dq.T


def tile_kernel(table, *refs, base):
    key_own, value_own, query_own, late_own, decoder = refs[0:5]
    fetch_x, fetch_z = refs[5:8], refs[8:11]
    late_x, late_z = refs[11:14], refs[14:17]
    send_x, own_z, send_z = refs[17], refs[18], refs[19:22]
    scratch = refs[22:]
    kv_rows, q_rows, g_rows, lse_rows, delta_rows, dq_rows, dk_acc, dv_acc = scratch
    sides = ((fetch_x, late_x), (fetch_z, late_z))
    channels = decoder.shape[1]
    head = pl.program_id(0) * 2 + base
    score_scale = 64 ** (-0.5)
    tn = (((0,), (1,)), ((), ()))

    def load(m):
        key_fetch = sides[m][0]
        query_fetch, late = sides[1 - m]
        for n in range(SIDE):
            kv_rows[n, 0] = key_own[m] if n == 0 else key_fetch[n - 1][0]
            kv_rows[n, 1] = value_own[m] if n == 0 else key_fetch[n - 1][1]
            q_rows[n] = query_own[m] if n == 0 else query_fetch[n - 1][2]
            package = late_own.at[m] if n == 0 else late[n - 1]
            g_rows[n] = lax.dot_general(
                package[:channels, :], decoder[...], tn, preferred_element_type=F32
            ).astype(BF16)
            stat = package[channels:, :].astype(F32)
            stat = stat[: stat.shape[0] // 2] + stat[stat.shape[0] // 2 :]
            lse_rows[n], delta_rows[n] = stat[:8], stat[8:]
            for i in range(2):
                lse_rows[n, i : i + 1, :], delta_rows[n, i : i + 1, :] = (
                    lse_rows[n, pl.ds(head + i, 1), :],
                    delta_rows[n, pl.ds(head + i, 1), :],
                )

    def store(m):
        def out(kind, n, value):
            if m == (1 if kind == 2 else 0):
                send_x[table[2, n], kind] = value.astype(BF16)
            elif n == 0:
                own_z[kind] = value
            else:
                send_z[n - 1][kind] = value.astype(BF16)

        for n in range(SIDE):
            out(0, n, dk_acc[n] * score_scale)
            out(1, n, dv_acc[n])
            out(2, n, dq_rows[n] * score_scale)

    def one_member(m, carry):
        for n in range(2):
            pl.when(m == n)(functools.partial(load, n))
        head_pair_tiles(table.at[m], scratch)
        for n in range(2):
            pl.when(m == n)(functools.partial(store, n))
        return carry

    lax.fori_loop(0, 2, one_member, 0)


def attention_tiles(half, tables, key_rows, value_rows, query, fetched_x, fetched_z, late_own, late_x, late_z, decoder_matrix):
    members, rows, width = key_rows.shape
    stats, channels = late_own.shape[1], decoder_matrix.shape[1]
    pairs = width // 256
    base = half * pairs
    own_spec = pl.BlockSpec((members, rows, 128), lambda h, tab: (0, 0, base + h))
    far_spec = pl.BlockSpec((3, rows, 128), lambda h, tab: (0, 0, h))
    late_spec = pl.BlockSpec((stats, rows), lambda h, tab: (0, 0))
    out = pl.pallas_call(
        functools.partial(tile_kernel, base=2 * base),
        out_shape=[
            pltpu.HBM((SIDE, 3, rows, width // 2), BF16),
            pltpu.HBM((3, rows, width // 2), F32),
        ]
        + [pltpu.HBM((3, rows, width // 2), BF16)] * 3,
        grid_spec=pltpu.PrefetchScalarGridSpec(
            num_scalar_prefetch=1,
            grid=(pairs,),
            in_specs=[own_spec] * 3
            + [
                pl.BlockSpec((members, stats, rows), lambda h, tab: (0, 0, 0)),
                pl.BlockSpec((128, channels), lambda h, tab: (base + h, 0)),
            ]
            + [far_spec] * 6
            + [late_spec] * 6,
            out_specs=[pl.BlockSpec((SIDE, 3, rows, 128), lambda h, tab: (0, 0, 0, h))]
            + [far_spec] * 4,
            scratch_shapes=[
                pltpu.VMEM((SIDE, 2, rows, 128), BF16),
                pltpu.VMEM((SIDE, rows, 128), BF16),
                pltpu.VMEM((SIDE, rows, 128), BF16),
                pltpu.VMEM((SIDE, 8, rows), F32),
                pltpu.VMEM((SIDE, 8, rows), F32),
                pltpu.VMEM((SIDE, rows, 128), F32),
                pltpu.VMEM((SIDE, rows, 128), F32),
                pltpu.VMEM((SIDE, rows, 128), F32),
            ],
        ),
        compiler_params=pltpu.CompilerParams(
            dimension_semantics=("arbitrary",), vmem_limit_bytes=50 * 1024 * 1024
        ),
        cost_estimate=pl.CostEstimate(
            flops=5 * 2 * (SIDE * SIDE * KB) * rows * 128 * 4 * pairs * members,
            transcendentals=SIDE * SIDE * KB * rows * 2 * pairs * members,
            bytes_accessed=20 * 1024 * 1024,
        ),
        name="attention_tiles",
    )(
        tables,
        *in_hbm(key_rows, value_rows, query, late_own, decoder_matrix),
        *in_hbm(*fetched_x, *fetched_z, *late_x, *late_z),
    )
    return out[0], out[1], out[2:]


def sum_kernel(got_x, own_z, *refs):
    got_z, outs = refs[:3], refs[-3:]
    for kind, ref in enumerate(outs):
        along_x = got_x[0, kind].astype(F32)
        for n in range(1, SIDE):
            along_x = along_x + got_x[n, kind].astype(F32)
        along_z = own_z[kind]
        for got in got_z:
            along_z = along_z + got[kind].astype(F32)
        ref[1 if kind == 2 else 0] = along_x
        ref[0 if kind == 2 else 1] = along_z


def summed(half, got_x, own_z, got_z, outs):
    _, rows, lanes = own_z.shape
    z_spec = pl.BlockSpec((3, rows // 2, lanes), lambda r: (0, r, 0))
    shape = jax.ShapeDtypeStruct((2, rows, 2 * lanes), F32)
    kept = list(outs) if outs else []
    return pl.pallas_call(
        sum_kernel,
        out_shape=[shape] * 3,
        grid=(2,),
        in_specs=[pl.BlockSpec((SIDE, 3, rows // 2, lanes), lambda r: (0, 0, r, 0))]
        + [z_spec] * 4
        + [pl.BlockSpec(memory_space=pl.ANY)] * len(kept),
        out_specs=[pl.BlockSpec((2, rows // 2, lanes), lambda r: (0, r, half))] * 3,
        input_output_aliases={5 + n: n for n in range(len(kept))},
        compiler_params=pltpu.CompilerParams(vmem_limit_bytes=50 * 1024 * 1024),
        name="summed",
    )(*in_hbm(got_x, own_z, *got_z), *kept)


def outgoing(half, key_rows, value_rows, query):
    lanes = query.shape[-1] // 2
    part = slice(half * lanes, (half + 1) * lanes)
    return [
        jnp.stack([key_rows[m, :, part], value_rows[m, :, part], query[1 - m, :, part]]) for m in range(2)
    ]


def in_hbm(*arrays):
    return [pltpu.with_memory_space_constraint(a, pltpu.HBM) for a in arrays]


def shards(
    hidden_embedding,
    decoder_matrix,
    baseline_field,
    truth_field,
    cell_surface_share,
    node_order,
    query,
    key_rows,
    value_rows,
    row_lse,
    kv_owner,
    kv_local,
):
    members, nodes, width = hidden_embedding.shape
    heads = row_lse.shape[1]
    x_at = lax.axis_index("x")
    z_at = lax.axis_index("z")

    own_0 = outgoing(0, key_rows, value_rows, query)
    near = [fetched(a, axis, d) for a, axis in zip(own_0, ("x", "z")) for d in (1, 3)]
    own_1 = outgoing(1, key_rows, value_rows, query)

    forecast = baseline_field[None] + jnp.einsum(
        "mou,ut->mto", hidden_embedding, decoder_matrix, preferred_element_type=F32
    )
    groups = lax.axis_size(MEMBER)
    span = nodes // groups
    channels = forecast.shape[1]
    offset = lax.axis_index(MEMBER) * span
    by_node = forecast.reshape(members, channels, groups, span).transpose(2, 1, 0, 3)
    everyone = lax.all_to_all(
        by_node.reshape(groups, channels, members * span), MEMBER, 0, 0, tiled=True
    )
    observed = lax.dynamic_slice_in_dim(truth_field, offset, span, 1)
    area = lax.dynamic_slice_in_dim(cell_surface_share, offset, span, 0)
    derivative = score_gradient(
        everyone, jnp.tile(observed, (1, members)), jnp.tile(area[None], (1, members))
    )
    derivative, own_1, near, decoder_rows = lax.optimization_barrier(
        (derivative, own_1, near, in_hbm(decoder_matrix)[0])
    )
    returned = lax.all_to_all(derivative, MEMBER, 0, 0, tiled=True)
    far = [fetched(near[0], "x", 1), fetched(near[2], "z", 1)]
    before = [fetched(a, axis, 3) for a, axis in zip(own_1, ("x", "z"))]
    returned, own_1, before = lax.optimization_barrier((returned, own_1, before))
    grad_forecast = (
        returned.reshape(groups, channels, members, span)
        .transpose(2, 1, 0, 3)
        .reshape(members, channels, nodes)
    )

    shard_ids = jnp.arange(SIDE * SIDE, dtype=jnp.int32)
    around = jnp.arange(SIDE, dtype=jnp.int32)
    named = jnp.sum(
        jnp.where(kv_owner[:, :, None] == shard_ids[None, None, :], kv_local[:, :, None], 0), axis=1
    ).reshape(SIDE, SIDE, SIDE, SIDE)
    x_near = ((x_at + around) % SIDE)[:, None] == around[None, :]
    z_near = ((z_at + around) % SIDE)[:, None] == around[None, :]
    x_here, z_here = x_near[0], z_near[0]

    def picked(sx, sz, ox, oz):
        chosen = (
            sx[:, None, None, None, :, None, None, None]
            & sz[None, :, None, None, None, :, None, None]
            & ox[None, None, :, None, None, None, :, None]
            & oz[None, None, None, :, None, None, None, :]
        )
        return jnp.sum(jnp.where(chosen, named, 0), axis=(4, 5, 6, 7)).reshape(-1)

    tables = jnp.stack(
        [
            picked(x_here[None], z_near, x_near, z_here[None]),
            picked(x_near, z_here[None], x_here[None], z_near),
            jnp.pad((x_at + around) % SIDE, (0, SIDE * (SIDE - 1))),
        ]
    )

    permuter = (node_order[0][:, None] == jnp.arange(nodes, dtype=jnp.int32)[None, :]).astype(BF16)
    grad_columns = jnp.einsum(
        "mcg,tg->mct", grad_forecast, permuter, preferred_element_type=F32
    ).astype(BF16)
    grad_latent = jnp.einsum(
        "wc,mct->mwt", decoder_matrix, grad_columns, preferred_element_type=F32
    ).astype(BF16)
    saved = jnp.einsum("mgw,tg->mwt", hidden_embedding, permuter, preferred_element_type=F32).astype(
        BF16
    )
    split = (members, heads, width // heads, nodes)
    delta = jnp.sum(
        grad_latent.astype(F32).reshape(split) * saved.astype(F32).reshape(split), axis=2
    )
    late_own = jnp.concatenate(
        [grad_columns] + [part[n] for n in range(2) for part in (two_parts(row_lse), two_parts(delta))],
        axis=1,
    )
    late_z = [fetched(late_own[0], "z", d) for d in (1, 2, 3)]
    late_x = [fetched(late_own[1], "x", d) for d in (1, 2, 3)]
    late_own, own_1, before = lax.optimization_barrier((late_own, own_1, before))
    after = [fetched(a, axis, 1) for a, axis in zip(own_1, ("x", "z"))]
    last = [fetched(a, axis, 3) for a, axis in zip(before, ("x", "z"))]
    came = (
        ((near[0], far[0], near[1]), (near[2], far[1], near[3])),
        ((after[0], last[0], before[0]), (after[1], last[1], before[1])),
    )

    outs = None
    parts = []
    for half in range(2):
        send_x, own, send_z = attention_tiles(
            half,
            tables,
            key_rows,
            value_rows,
            query,
            *came[half],
            late_own,
            late_x,
            late_z,
            decoder_rows,
        )
        if parts:
            (first_x, first_own, first_z) = parts[0]
            send_x, send_z, first_x, first_z = lax.optimization_barrier(
                (send_x, send_z, first_x, first_z)
            )
            parts[0] = (first_x, first_own, first_z)
        got_x = lax.all_to_all(send_x, "x", 0, 0, tiled=True)
        got_z = [delivered(send_z[d - 1], "z", d) for d in (1, 2, 3)]
        parts.append((got_x, own, got_z))
    for half, part in enumerate(parts):
        outs = summed(half, *part, outs)
    grad_key, grad_value, grad_query = outs
    return grad_query, grad_key, grad_value


def solution(mesh):
    finer = Mesh(mesh.devices.reshape(4, 2, SIDE, SIDE), ("y", "core", "x", "z"))
    plane = ("x", "z")
    in_specs = (
        P(MEMBER, plane, None),
        P(),
        P(None, plane),
        P(None, plane),
        P(plane),
        P(plane, None),
        P(MEMBER, plane, None),
        P(MEMBER, plane, None),
        P(MEMBER, plane, None),
        P(MEMBER, None, plane),
        P(),
        P(),
    )
    out_specs = (P(MEMBER, plane, None), P(MEMBER, plane, None), P(MEMBER, plane, None))
    return jax.shard_map(
        shards, mesh=finer, in_specs=in_specs, out_specs=out_specs, check_vma=False
    )
```

```python
import functools
import math

import jax
import jax.numpy as jnp
from jax import lax
from jax.experimental import pallas as pl
from jax.experimental.pallas import tpu as pltpu
from jax.sharding import Mesh
from jax.sharding import PartitionSpec as P

KB = 128
SIDE = 4
GROUP = 2
MEMBER = ("y", "core")
LOSS_SCALE = 4096.0
FAIR_EPS = 0.05
NORM_EPS = 1e-06
LOG2E = math.log2(math.e)
F32 = jnp.float32
BF16 = jnp.bfloat16


def score_kernel(forecast_ref, truth_ref, area_ref, out_ref, swapped_ref):
    groups, _, lanes = forecast_ref.shape
    count = 2 * groups
    for k in range(groups):
        swapped_ref[k] = pltpu.roll(forecast_ref[k], lanes // 2, 1)
    weight = LOSS_SCALE * area_ref[...]

    def unit(x):
        return x * (1.0 / jnp.sqrt(jnp.sum(x * x, axis=0, keepdims=True) + NORM_EPS))

    def one_group(j, carry):
        one = forecast_ref[j]
        total = jnp.zeros_like(one)
        for k in range(groups):
            total = total + unit(one - forecast_ref[k]) + unit(one - swapped_ref[k])
        gradient = weight * (
            unit(one - truth_ref[...]) / count - (1.0 - FAIR_EPS) / (count * (count - 1)) * total
        )
        out_ref[j] = gradient.astype(BF16)
        return carry

    lax.fori_loop(0, groups, one_group, 0)


def score_gradient(forecasts, truth, area):
    return pl.pallas_call(
        score_kernel,
        out_shape=jax.ShapeDtypeStruct(forecasts.shape, BF16),
        in_specs=[pl.BlockSpec(memory_space=pltpu.VMEM)] * 3,
        out_specs=pl.BlockSpec(memory_space=pltpu.VMEM),
        scratch_shapes=[pltpu.VMEM(forecasts.shape, F32)],
        name="score_gradient",
    )(forecasts, truth, area)


def two_parts(x):
    high = x.astype(BF16)
    return [high, (x - lax.reduce_precision(x, 8, 7)).astype(BF16)]


def fetched(x, axis, distance):
    return lax.ppermute(x, axis, [(i, (i - distance) % SIDE) for i in range(SIDE)])


def delivered(x, axis, distance):
    return lax.ppermute(x, axis, [(i, (i + distance) % SIDE) for i in range(SIDE)])


def head_pair_tiles(table, scratch):
    kv_rows, q_rows, g_rows, lse_rows, delta_rows, dq_rows, dk_acc, dv_acc = scratch
    head_dim = 64
    score_scale = head_dim ** (-0.5)
    keys = GROUP * KB
    first = lax.broadcasted_iota(jnp.int32, (keys, 2 * head_dim), 1) < head_dim
    nt = (((1,), (1,)), ((), ()))
    dk_acc[...] = jnp.zeros_like(dk_acc)
    dv_acc[...] = jnp.zeros_like(dv_acc)

    def by_head(x):
        x = x.astype(F32)
        return jnp.concatenate(
            [jnp.where(first, x, 0.0).astype(BF16), jnp.where(first, 0.0, x).astype(BF16)], axis=0
        )

    for t in range(SIDE):
        q, g = q_rows[t], g_rows[t]
        dq = None
        for start in range(0, SIDE, GROUP):
            group = range(start, start + GROUP)
            starts = [pl.multiple_of(table[t * SIDE + a] * KB, KB) for a in group]
            k, v = (
                by_head(
                    jnp.concatenate([kv_rows[a, i, pl.ds(s, KB), :] for a, s in zip(group, starts)], axis=0)
                )
                for i in range(2)
            )
            scores = lax.dot_general(k, q, nt, preferred_element_type=F32)
            dp = lax.dot_general(v, g, nt, preferred_element_type=F32)
            ps, dss = [], []
            for n in range(2):
                part = slice(n * keys, (n + 1) * keys)
                p = jnp.exp2(scores[part] * (score_scale * LOG2E) - lse_rows[t, n : n + 1, :] * LOG2E)
                ps.append(p.astype(BF16))
                dss.append((p * (dp[part] - delta_rows[t, n : n + 1, :])).astype(BF16))
            p, ds = jnp.concatenate(ps, axis=0), jnp.concatenate(dss, axis=0)
            dv = jnp.dot(p, g, preferred_element_type=F32)
            dk = jnp.dot(ds, q, preferred_element_type=F32)
            dv = jnp.where(first, dv[:keys], dv[keys:])
            dk = jnp.where(first, dk[:keys], dk[keys:])
            for n, (a, s) in enumerate(zip(group, starts)):
                dv_acc[a, pl.ds(s, KB), :] += dv[n * KB : (n + 1) * KB]
                dk_acc[a, pl.ds(s, KB), :] += dk[n * KB : (n + 1) * KB]
            part = jnp.dot(k.T, ds, preferred_element_type=F32)
            dq = part if dq is None else dq + part
        dq_rows[t] = dq.T


def tile_kernel(table, *refs, base):
    key_own, value_own, query_own, late_own, decoder = refs[0:5]
    fetch_x, fetch_z = refs[5:8], refs[8:11]
    late_x, late_z = refs[11:14], refs[14:17]
    send_x, own_z, send_z = refs[17], refs[18], refs[19:22]
    scratch = refs[22:]
    kv_rows, q_rows, g_rows, lse_rows, delta_rows, dq_rows, dk_acc, dv_acc = scratch
    sides = ((fetch_x, late_x), (fetch_z, late_z))
    channels = decoder.shape[0]
    head = pl.program_id(0) * 2 + base
    score_scale = 64 ** (-0.5)
    tn = (((0,), (0,)), ((), ()))

    def load(m):
        key_fetch = sides[m][0]
        query_fetch, late = sides[1 - m]
        for n in range(SIDE):
            kv_rows[n, 0] = key_own[m] if n == 0 else key_fetch[n - 1][0]
            kv_rows[n, 1] = value_own[m] if n == 0 else key_fetch[n - 1][1]
            q_rows[n] = query_own[m] if n == 0 else query_fetch[n - 1][2]
            package = late_own.at[m] if n == 0 else late[n - 1]
            g_rows[n] = lax.dot_general(
                package[:channels, :], decoder[...], tn, preferred_element_type=F32
            ).astype(BF16)
            stat = package[channels:, :].astype(F32)
            stat = stat[: stat.shape[0] // 2] + stat[stat.shape[0] // 2 :]
            lse_rows[n], delta_rows[n] = stat[:8], stat[8:]
            for i in range(2):
                lse_rows[n, i : i + 1, :], delta_rows[n, i : i + 1, :] = (
                    lse_rows[n, pl.ds(head + i, 1), :],
                    delta_rows[n, pl.ds(head + i, 1), :],
                )

    def store(m):
        def out(kind, n, value):
            if m == (1 if kind == 2 else 0):
                send_x[table[2, n], kind] = value.astype(BF16)
            elif n == 0:
                own_z[kind] = value
            else:
                send_z[n - 1][kind] = value.astype(BF16)

        for n in range(SIDE):
            out(0, n, dk_acc[n] * score_scale)
            out(1, n, dv_acc[n])
            out(2, n, dq_rows[n] * score_scale)

    def one_member(m, carry):
        for n in range(2):
            pl.when(m == n)(functools.partial(load, n))
        head_pair_tiles(table.at[m], scratch)
        for n in range(2):
            pl.when(m == n)(functools.partial(store, n))
        return carry

    lax.fori_loop(0, 2, one_member, 0)


def attention_tiles(half, tables, key_rows, value_rows, query, fetched_x, fetched_z, late_own, late_x, late_z, decoder_matrix):
    members, rows, width = key_rows.shape
    stats, channels = late_own.shape[1], decoder_matrix.shape[0]
    pairs = width // 256
    base = half * pairs
    own_spec = pl.BlockSpec((members, rows, 128), lambda h, tab: (0, 0, base + h))
    far_spec = pl.BlockSpec((3, rows, 128), lambda h, tab: (0, 0, h))
    late_spec = pl.BlockSpec((stats, rows), lambda h, tab: (0, 0))
    out = pl.pallas_call(
        functools.partial(tile_kernel, base=2 * base),
        out_shape=[
            pltpu.HBM((SIDE, 3, rows, width // 2), BF16),
            pltpu.HBM((3, rows, width // 2), F32),
        ]
        + [pltpu.HBM((3, rows, width // 2), BF16)] * 3,
        grid_spec=pltpu.PrefetchScalarGridSpec(
            num_scalar_prefetch=1,
            grid=(pairs,),
            in_specs=[own_spec] * 3
            + [
                pl.BlockSpec((members, stats, rows), lambda h, tab: (0, 0, 0)),
                pl.BlockSpec((channels, 128), lambda h, tab: (0, base + h)),
            ]
            + [far_spec] * 6
            + [late_spec] * 6,
            out_specs=[pl.BlockSpec((SIDE, 3, rows, 128), lambda h, tab: (0, 0, 0, h))]
            + [far_spec] * 4,
            scratch_shapes=[
                pltpu.VMEM((SIDE, 2, rows, 128), BF16),
                pltpu.VMEM((SIDE, rows, 128), BF16),
                pltpu.VMEM((SIDE, rows, 128), BF16),
                pltpu.VMEM((SIDE, 8, rows), F32),
                pltpu.VMEM((SIDE, 8, rows), F32),
                pltpu.VMEM((SIDE, rows, 128), F32),
                pltpu.VMEM((SIDE, rows, 128), F32),
                pltpu.VMEM((SIDE, rows, 128), F32),
            ],
        ),
        compiler_params=pltpu.CompilerParams(
            dimension_semantics=("arbitrary",), vmem_limit_bytes=50 * 1024 * 1024
        ),
        cost_estimate=pl.CostEstimate(
            flops=5 * 2 * (SIDE * SIDE * KB) * rows * 128 * 4 * pairs * members,
            transcendentals=SIDE * SIDE * KB * rows * 2 * pairs * members,
            bytes_accessed=20 * 1024 * 1024,
        ),
        name="attention_tiles",
    )(
        tables,
        *in_hbm(key_rows, value_rows, query, late_own, decoder_matrix),
        *in_hbm(*fetched_x, *fetched_z, *late_x, *late_z),
    )
    return out[0], out[1], out[2:]


def sum_kernel(got_x, own_z, *refs):
    got_z, outs = refs[:3], refs[-3:]
    for kind, ref in enumerate(outs):
        along_x = got_x[0, kind].astype(F32)
        for n in range(1, SIDE):
            along_x = along_x + got_x[n, kind].astype(F32)
        along_z = own_z[kind]
        for got in got_z:
            along_z = along_z + got[kind].astype(F32)
        ref[1 if kind == 2 else 0] = along_x
        ref[0 if kind == 2 else 1] = along_z


def summed(half, got_x, own_z, got_z, outs):
    _, rows, lanes = own_z.shape
    z_spec = pl.BlockSpec((3, rows // 2, lanes), lambda r: (0, r, 0))
    shape = jax.ShapeDtypeStruct((2, rows, 2 * lanes), F32)
    kept = list(outs) if outs else []
    return pl.pallas_call(
        sum_kernel,
        out_shape=[shape] * 3,
        grid=(2,),
        in_specs=[pl.BlockSpec((SIDE, 3, rows // 2, lanes), lambda r: (0, 0, r, 0))]
        + [z_spec] * 4
        + [pl.BlockSpec(memory_space=pl.ANY)] * len(kept),
        out_specs=[pl.BlockSpec((2, rows // 2, lanes), lambda r: (0, r, half))] * 3,
        input_output_aliases={5 + n: n for n in range(len(kept))},
        compiler_params=pltpu.CompilerParams(vmem_limit_bytes=50 * 1024 * 1024),
        name="summed",
    )(*in_hbm(got_x, own_z, *got_z), *kept)


def pack_kernel(key_rows, value_rows, query, along_x, along_z):
    for m, out in enumerate((along_x, along_z)):
        out[0] = key_rows[m]
        out[1] = value_rows[m]
        out[2] = query[1 - m]


def outgoing(half, key_rows, value_rows, query):
    members, rows, width = query.shape
    lanes = width // 2
    block = pl.BlockSpec((members, rows // 4, lanes), lambda r: (0, r, half))
    return pl.pallas_call(
        pack_kernel,
        out_shape=[pltpu.HBM((3, rows, lanes), BF16)] * 2,
        grid=(4,),
        in_specs=[block] * 3,
        out_specs=[pl.BlockSpec((3, rows // 4, lanes), lambda r: (0, r, 0))] * 2,
        name="outgoing",
    )(*in_hbm(key_rows, value_rows, query))


def in_hbm(*arrays):
    return [pltpu.with_memory_space_constraint(a, pltpu.HBM) for a in arrays]


def shards(
    hidden_embedding,
    decoder_matrix,
    baseline_field,
    truth_field,
    cell_surface_share,
    node_order,
    query,
    key_rows,
    value_rows,
    row_lse,
    kv_owner,
    kv_local,
):
    members, nodes, width = hidden_embedding.shape
    heads = row_lse.shape[1]
    x_at = lax.axis_index("x")
    z_at = lax.axis_index("z")

    own_0 = outgoing(0, key_rows, value_rows, query)
    near = [fetched(a, axis, d) for a, axis in zip(own_0, ("x", "z")) for d in (1, 3)]
    own_1 = outgoing(1, key_rows, value_rows, query)

    forecast = baseline_field[None] + jnp.einsum(
        "mou,ut->mto", hidden_embedding, decoder_matrix, preferred_element_type=F32
    )
    groups = lax.axis_size(MEMBER)
    span = nodes // groups
    channels = forecast.shape[1]
    offset = lax.axis_index(MEMBER) * span
    by_node = forecast.reshape(members, channels, groups, span).transpose(2, 1, 0, 3)
    everyone = lax.all_to_all(
        by_node.reshape(groups, channels, members * span), MEMBER, 0, 0, tiled=True
    )
    observed = lax.dynamic_slice_in_dim(truth_field, offset, span, 1)
    area = lax.dynamic_slice_in_dim(cell_surface_share, offset, span, 0)
    derivative = score_gradient(
        everyone, jnp.tile(observed, (1, members)), jnp.tile(area[None], (1, members))
    )
    derivative, own_1, near, decoder_rows = lax.optimization_barrier(
        (derivative, own_1, near, decoder_matrix.T)
    )
    returned = lax.all_to_all(derivative, MEMBER, 0, 0, tiled=True)
    far = [fetched(near[0], "x", 1), fetched(near[2], "z", 1)]
    before = [fetched(a, axis, 3) for a, axis in zip(own_1, ("x", "z"))]
    grad_forecast = (
        returned.reshape(groups, channels, members, span)
        .transpose(2, 1, 0, 3)
        .reshape(members, channels, nodes)
    )

    shard_ids = jnp.arange(SIDE * SIDE, dtype=jnp.int32)
    around = jnp.arange(SIDE, dtype=jnp.int32)
    named = jnp.sum(
        jnp.where(kv_owner[:, :, None] == shard_ids[None, None, :], kv_local[:, :, None], 0), axis=1
    ).reshape(SIDE, SIDE, SIDE, SIDE)
    x_near = ((x_at + around) % SIDE)[:, None] == around[None, :]
    z_near = ((z_at + around) % SIDE)[:, None] == around[None, :]
    x_here, z_here = x_near[0], z_near[0]

    def picked(sx, sz, ox, oz):
        chosen = (
            sx[:, None, None, None, :, None, None, None]
            & sz[None, :, None, None, None, :, None, None]
            & ox[None, None, :, None, None, None, :, None]
            & oz[None, None, None, :, None, None, None, :]
        )
        return jnp.sum(jnp.where(chosen, named, 0), axis=(4, 5, 6, 7)).reshape(-1)

    tables = jnp.stack(
        [
            picked(x_here[None], z_near, x_near, z_here[None]),
            picked(x_near, z_here[None], x_here[None], z_near),
            jnp.pad((x_at + around) % SIDE, (0, SIDE * (SIDE - 1))),
        ]
    )

    permuter = (node_order[0][:, None] == jnp.arange(nodes, dtype=jnp.int32)[None, :]).astype(BF16)
    grad_columns = jnp.einsum(
        "mcg,tg->mct", grad_forecast, permuter, preferred_element_type=F32
    ).astype(BF16)
    grad_latent = jnp.einsum(
        "wc,mct->mwt", decoder_matrix, grad_columns, preferred_element_type=F32
    ).astype(BF16)
    saved = jnp.einsum("mgw,tg->mwt", hidden_embedding, permuter, preferred_element_type=F32).astype(
        BF16
    )
    split = (members, heads, width // heads, nodes)
    delta = jnp.sum(
        grad_latent.astype(F32).reshape(split) * saved.astype(F32).reshape(split), axis=2
    )
    late_own = jnp.concatenate(
        [grad_columns] + [part[n] for n in range(2) for part in (two_parts(row_lse), two_parts(delta))],
        axis=1,
    )
    late_own, own_1, before, far = lax.optimization_barrier((late_own, own_1, before, far))
    late_z = [fetched(late_own[0], "z", d) for d in (1, 2, 3)]
    late_x = [fetched(late_own[1], "x", d) for d in (1, 2, 3)]
    late_own, own_1, before = lax.optimization_barrier((late_own, own_1, before))
    after = [fetched(a, axis, 1) for a, axis in zip(own_1, ("x", "z"))]
    last = [fetched(a, axis, 3) for a, axis in zip(before, ("x", "z"))]
    came = (
        ((near[0], far[0], near[1]), (near[2], far[1], near[3])),
        ((after[0], last[0], before[0]), (after[1], last[1], before[1])),
    )

    outs = None
    parts = []
    for half in range(2):
        send_x, own, send_z = attention_tiles(
            half,
            tables,
            key_rows,
            value_rows,
            query,
            *came[half],
            late_own,
            late_x,
            late_z,
            decoder_rows,
        )
        if parts:
            (first_x, first_own, first_z) = parts[0]
            send_x, send_z, first_x, first_z = lax.optimization_barrier(
                (send_x, send_z, first_x, first_z)
            )
            parts[0] = (first_x, first_own, first_z)
        got_x = lax.all_to_all(send_x, "x", 0, 0, tiled=True)
        got_z = [delivered(send_z[d - 1], "z", d) for d in (1, 2, 3)]
        parts.append((got_x, own, got_z))
    for half, part in enumerate(parts):
        outs = summed(half, *part, outs)
    grad_key, grad_value, grad_query = outs
    return grad_query, grad_key, grad_value


def solution(mesh):
    finer = Mesh(mesh.devices.reshape(4, 2, SIDE, SIDE), ("y", "core", "x", "z"))
    plane = ("x", "z")
    in_specs = (
        P(MEMBER, plane, None),
        P(),
        P(None, plane),
        P(None, plane),
        P(plane),
        P(plane, None),
        P(MEMBER, plane, None),
        P(MEMBER, plane, None),
        P(MEMBER, plane, None),
        P(MEMBER, None, plane),
        P(),
        P(),
    )
    out_specs = (P(MEMBER, plane, None), P(MEMBER, plane, None), P(MEMBER, plane, None))
    return jax.shard_map(
        shards, mesh=finer, in_specs=in_specs, out_specs=out_specs, check_vma=False
    )
```

```python
import functools
import math

import jax
import jax.numpy as jnp
from jax import lax
from jax.experimental import pallas as pl
from jax.experimental.pallas import tpu as pltpu
from jax.sharding import Mesh
from jax.sharding import PartitionSpec as P

KB = 128
SIDE = 4
GROUP = 2
MEMBER = ("y", "core")
LOSS_SCALE = 4096.0
FAIR_EPS = 0.05
NORM_EPS = 1e-06
LOG2E = math.log2(math.e)
F32 = jnp.float32
BF16 = jnp.bfloat16


def score_kernel(forecast_ref, truth_ref, area_ref, out_ref, swapped_ref):
    groups, _, lanes = forecast_ref.shape
    count = 2 * groups
    for k in range(groups):
        swapped_ref[k] = pltpu.roll(forecast_ref[k], lanes // 2, 1)
    weight = LOSS_SCALE * area_ref[...]

    def unit(x):
        return x * (1.0 / jnp.sqrt(jnp.sum(x * x, axis=0, keepdims=True) + NORM_EPS))

    def one_group(j, carry):
        one = forecast_ref[j]
        total = jnp.zeros_like(one)
        for k in range(groups):
            total = total + unit(one - forecast_ref[k]) + unit(one - swapped_ref[k])
        gradient = weight * (
            unit(one - truth_ref[...]) / count - (1.0 - FAIR_EPS) / (count * (count - 1)) * total
        )
        out_ref[j] = gradient.astype(BF16)
        return carry

    lax.fori_loop(0, groups, one_group, 0)


def score_gradient(forecasts, truth, area):
    return pl.pallas_call(
        score_kernel,
        out_shape=jax.ShapeDtypeStruct(forecasts.shape, BF16),
        in_specs=[pl.BlockSpec(memory_space=pltpu.VMEM)] * 3,
        out_specs=pl.BlockSpec(memory_space=pltpu.VMEM),
        scratch_shapes=[pltpu.VMEM(forecasts.shape, F32)],
        name="score_gradient",
    )(forecasts, truth, area)


def two_parts(x):
    high = x.astype(BF16)
    return [high, (x - lax.reduce_precision(x, 8, 7)).astype(BF16)]


def fetched(x, axis, distance):
    return lax.ppermute(x, axis, [(i, (i - distance) % SIDE) for i in range(SIDE)])


def delivered(x, axis, distance):
    return lax.ppermute(x, axis, [(i, (i + distance) % SIDE) for i in range(SIDE)])


def head_pair_tiles(table, scratch):
    kv_rows, q_rows, g_rows, lse_rows, delta_rows, dq_rows, dk_acc, dv_acc = scratch
    head_dim = 64
    score_scale = head_dim ** (-0.5)
    keys = GROUP * KB
    first = lax.broadcasted_iota(jnp.int32, (keys, 2 * head_dim), 1) < head_dim
    nt = (((1,), (1,)), ((), ()))
    dk_acc[...] = jnp.zeros_like(dk_acc)
    dv_acc[...] = jnp.zeros_like(dv_acc)

    def by_head(x):
        x = x.astype(F32)
        return jnp.concatenate(
            [jnp.where(first, x, 0.0).astype(BF16), jnp.where(first, 0.0, x).astype(BF16)], axis=0
        )

    for t in range(SIDE):
        q, g = q_rows[t], g_rows[t]
        dq = None
        for start in range(0, SIDE, GROUP):
            group = range(start, start + GROUP)
            starts = [pl.multiple_of(table[t * SIDE + a] * KB, KB) for a in group]
            k, v = (
                by_head(
                    jnp.concatenate([kv_rows[a, i, pl.ds(s, KB), :] for a, s in zip(group, starts)], axis=0)
                )
                for i in range(2)
            )
            scores = lax.dot_general(k, q, nt, preferred_element_type=F32)
            dp = lax.dot_general(v, g, nt, preferred_element_type=F32)
            ps, dss = [], []
            for n in range(2):
                part = slice(n * keys, (n + 1) * keys)
                p = jnp.exp2(scores[part] * (score_scale * LOG2E) - lse_rows[t, n : n + 1, :] * LOG2E)
                ps.append(p.astype(BF16))
                dss.append((p * (dp[part] - delta_rows[t, n : n + 1, :])).astype(BF16))
            p, ds = jnp.concatenate(ps, axis=0), jnp.concatenate(dss, axis=0)
            dv = jnp.dot(p, g, preferred_element_type=F32)
            dk = jnp.dot(ds, q, preferred_element_type=F32)
            dv = jnp.where(first, dv[:keys], dv[keys:])
            dk = jnp.where(first, dk[:keys], dk[keys:])
            for n, (a, s) in enumerate(zip(group, starts)):
                dv_acc[a, pl.ds(s, KB), :] += dv[n * KB : (n + 1) * KB]
                dk_acc[a, pl.ds(s, KB), :] += dk[n * KB : (n + 1) * KB]
            part = jnp.dot(k.T, ds, preferred_element_type=F32)
            dq = part if dq is None else dq + part
        dq_rows[t] = dq.T


def tile_kernel(table, *refs, base):
    key_own, value_own, query_own, late_own, decoder = refs[0:5]
    fetch_x, fetch_z = refs[5:8], refs[8:11]
    late_x, late_z = refs[11:14], refs[14:17]
    send_x, own_z, send_z = refs[17], refs[18], refs[19:22]
    scratch = refs[22:]
    kv_rows, q_rows, g_rows, lse_rows, delta_rows, dq_rows, dk_acc, dv_acc = scratch
    sides = ((fetch_x, late_x), (fetch_z, late_z))
    channels = decoder.shape[0]
    head = pl.program_id(0) * 2 + base
    score_scale = 64 ** (-0.5)
    tn = (((0,), (0,)), ((), ()))

    def load(m):
        key_fetch = sides[m][0]
        query_fetch, late = sides[1 - m]
        for n in range(SIDE):
            kv_rows[n, 0] = key_own[m] if n == 0 else key_fetch[n - 1][0]
            kv_rows[n, 1] = value_own[m] if n == 0 else key_fetch[n - 1][1]
            q_rows[n] = query_own[m] if n == 0 else query_fetch[n - 1][2]
            package = late_own.at[m] if n == 0 else late[n - 1]
            g_rows[n] = lax.dot_general(
                package[:channels, :], decoder[...], tn, preferred_element_type=F32
            ).astype(BF16)
            stat = package[channels:, :].astype(F32)
            stat = stat[: stat.shape[0] // 2] + stat[stat.shape[0] // 2 :]
            lse_rows[n], delta_rows[n] = stat[:8], stat[8:]
            for i in range(2):
                lse_rows[n, i : i + 1, :], delta_rows[n, i : i + 1, :] = (
                    lse_rows[n, pl.ds(head + i, 1), :],
                    delta_rows[n, pl.ds(head + i, 1), :],
                )

    def store(m):
        def out(kind, n, value):
            if m == (1 if kind == 2 else 0):
                send_x[table[2, n], kind] = value.astype(BF16)
            elif n == 0:
                own_z[kind] = value
            else:
                send_z[n - 1][kind] = value.astype(BF16)

        for n in range(SIDE):
            out(0, n, dk_acc[n] * score_scale)
            out(1, n, dv_acc[n])
            out(2, n, dq_rows[n] * score_scale)

    def one_member(m, carry):
        for n in range(2):
            pl.when(m == n)(functools.partial(load, n))
        head_pair_tiles(table.at[m], scratch)
        for n in range(2):
            pl.when(m == n)(functools.partial(store, n))
        return carry

    lax.fori_loop(0, 2, one_member, 0)


def attention_tiles(half, tables, key_rows, value_rows, query, fetched_x, fetched_z, late_own, late_x, late_z, decoder_matrix):
    members, rows, width = key_rows.shape
    stats, channels = late_own.shape[1], decoder_matrix.shape[0]
    pairs = width // 256
    base = half * pairs
    own_spec = pl.BlockSpec((members, rows, 128), lambda h, tab: (0, 0, base + h))
    far_spec = pl.BlockSpec((3, rows, 128), lambda h, tab: (0, 0, h))
    late_spec = pl.BlockSpec((stats, rows), lambda h, tab: (0, 0))
    out = pl.pallas_call(
        functools.partial(tile_kernel, base=2 * base),
        out_shape=[
            pltpu.HBM((SIDE, 3, rows, width // 2), BF16),
            pltpu.HBM((3, rows, width // 2), F32),
        ]
        + [pltpu.HBM((3, rows, width // 2), BF16)] * 3,
        grid_spec=pltpu.PrefetchScalarGridSpec(
            num_scalar_prefetch=1,
            grid=(pairs,),
            in_specs=[own_spec] * 3
            + [
                pl.BlockSpec((members, stats, rows), lambda h, tab: (0, 0, 0)),
                pl.BlockSpec((channels, 128), lambda h, tab: (0, base + h)),
            ]
            + [far_spec] * 6
            + [late_spec] * 6,
            out_specs=[pl.BlockSpec((SIDE, 3, rows, 128), lambda h, tab: (0, 0, 0, h))]
            + [far_spec] * 4,
            scratch_shapes=[
                pltpu.VMEM((SIDE, 2, rows, 128), BF16),
                pltpu.VMEM((SIDE, rows, 128), BF16),
                pltpu.VMEM((SIDE, rows, 128), BF16),
                pltpu.VMEM((SIDE, 8, rows), F32),
                pltpu.VMEM((SIDE, 8, rows), F32),
                pltpu.VMEM((SIDE, rows, 128), F32),
                pltpu.VMEM((SIDE, rows, 128), F32),
                pltpu.VMEM((SIDE, rows, 128), F32),
            ],
        ),
        compiler_params=pltpu.CompilerParams(
            dimension_semantics=("arbitrary",), vmem_limit_bytes=50 * 1024 * 1024
        ),
        cost_estimate=pl.CostEstimate(
            flops=5 * 2 * (SIDE * SIDE * KB) * rows * 128 * 4 * pairs * members,
            transcendentals=SIDE * SIDE * KB * rows * 2 * pairs * members,
            bytes_accessed=20 * 1024 * 1024,
        ),
        name="attention_tiles",
    )(
        tables,
        *in_hbm(key_rows, value_rows, query, late_own, decoder_matrix),
        *in_hbm(*fetched_x, *fetched_z, *late_x, *late_z),
    )
    return out[0], out[1], out[2:]


def sum_kernel(got_x, own_z, *refs):
    got_z, outs = refs[:3], refs[-3:]
    for kind, ref in enumerate(outs):
        along_x = got_x[0, kind].astype(F32)
        for n in range(1, SIDE):
            along_x = along_x + got_x[n, kind].astype(F32)
        along_z = own_z[kind]
        for got in got_z:
            along_z = along_z + got[kind].astype(F32)
        ref[1 if kind == 2 else 0] = along_x
        ref[0 if kind == 2 else 1] = along_z


def summed(half, got_x, own_z, got_z, outs):
    _, rows, lanes = own_z.shape
    z_spec = pl.BlockSpec((3, rows // 2, lanes), lambda r: (0, r, 0))
    shape = jax.ShapeDtypeStruct((2, rows, 2 * lanes), F32)
    kept = list(outs) if outs else []
    return pl.pallas_call(
        sum_kernel,
        out_shape=[shape] * 3,
        grid=(2,),
        in_specs=[pl.BlockSpec((SIDE, 3, rows // 2, lanes), lambda r: (0, 0, r, 0))]
        + [z_spec] * 4
        + [pl.BlockSpec(memory_space=pl.ANY)] * len(kept),
        out_specs=[pl.BlockSpec((2, rows // 2, lanes), lambda r: (0, r, half))] * 3,
        input_output_aliases={5 + n: n for n in range(len(kept))},
        compiler_params=pltpu.CompilerParams(vmem_limit_bytes=50 * 1024 * 1024),
        name="summed",
    )(*in_hbm(got_x, own_z, *got_z), *kept)


def pack_kernel(key_rows, value_rows, query, along_x, along_z):
    for m, out in enumerate((along_x, along_z)):
        out[0] = key_rows[m]
        out[1] = value_rows[m]
        out[2] = query[1 - m]


def outgoing(half, key_rows, value_rows, query):
    members, rows, width = query.shape
    lanes = width // 2
    block = pl.BlockSpec((members, rows // 4, lanes), lambda r: (0, r, half))
    return pl.pallas_call(
        pack_kernel,
        out_shape=[pltpu.HBM((3, rows, lanes), BF16)] * 2,
        grid=(4,),
        in_specs=[block] * 3,
        out_specs=[pl.BlockSpec((3, rows // 4, lanes), lambda r: (0, r, 0))] * 2,
        name="outgoing",
    )(*in_hbm(key_rows, value_rows, query))


def in_hbm(*arrays):
    return [pltpu.with_memory_space_constraint(a, pltpu.HBM) for a in arrays]


def shards(
    hidden_embedding,
    decoder_matrix,
    baseline_field,
    truth_field,
    cell_surface_share,
    node_order,
    query,
    key_rows,
    value_rows,
    row_lse,
    kv_owner,
    kv_local,
):
    members, nodes, width = hidden_embedding.shape
    heads = row_lse.shape[1]
    x_at = lax.axis_index("x")
    z_at = lax.axis_index("z")

    own_0 = outgoing(0, key_rows, value_rows, query)
    near = [fetched(a, axis, d) for a, axis in zip(own_0, ("x", "z")) for d in (1, 3)]
    own_1 = outgoing(1, key_rows, value_rows, query)

    forecast = baseline_field[None] + jnp.einsum(
        "mou,ut->mto", hidden_embedding, decoder_matrix, preferred_element_type=F32
    )
    groups = lax.axis_size(MEMBER)
    span = nodes // groups
    channels = forecast.shape[1]
    offset = lax.axis_index(MEMBER) * span
    by_node = forecast.reshape(members, channels, groups, span).transpose(2, 1, 0, 3)
    everyone = lax.all_to_all(
        by_node.reshape(groups, channels, members * span), MEMBER, 0, 0, tiled=True
    )
    everyone, own_1, near = lax.optimization_barrier((everyone, own_1, near))
    far = [fetched(near[0], "x", 1), fetched(near[2], "z", 1)]
    before = [fetched(a, axis, 3) for a, axis in zip(own_1, ("x", "z"))]
    observed = lax.dynamic_slice_in_dim(truth_field, offset, span, 1)
    area = lax.dynamic_slice_in_dim(cell_surface_share, offset, span, 0)
    derivative = score_gradient(
        everyone, jnp.tile(observed, (1, members)), jnp.tile(area[None], (1, members))
    )
    returned = lax.all_to_all(derivative, MEMBER, 0, 0, tiled=True)
    returned, own_1, before, far = lax.optimization_barrier((returned, own_1, before, far))
    grad_forecast = (
        returned.reshape(groups, channels, members, span)
        .transpose(2, 1, 0, 3)
        .reshape(members, channels, nodes)
    )

    shard_ids = jnp.arange(SIDE * SIDE, dtype=jnp.int32)
    around = jnp.arange(SIDE, dtype=jnp.int32)
    named = jnp.sum(
        jnp.where(kv_owner[:, :, None] == shard_ids[None, None, :], kv_local[:, :, None], 0), axis=1
    ).reshape(SIDE, SIDE, SIDE, SIDE)
    x_near = ((x_at + around) % SIDE)[:, None] == around[None, :]
    z_near = ((z_at + around) % SIDE)[:, None] == around[None, :]
    x_here, z_here = x_near[0], z_near[0]

    def picked(sx, sz, ox, oz):
        chosen = (
            sx[:, None, None, None, :, None, None, None]
            & sz[None, :, None, None, None, :, None, None]
            & ox[None, None, :, None, None, None, :, None]
            & oz[None, None, None, :, None, None, None, :]
        )
        return jnp.sum(jnp.where(chosen, named, 0), axis=(4, 5, 6, 7)).reshape(-1)

    tables = jnp.stack(
        [
            picked(x_here[None], z_near, x_near, z_here[None]),
            picked(x_near, z_here[None], x_here[None], z_near),
            jnp.pad((x_at + around) % SIDE, (0, SIDE * (SIDE - 1))),
        ]
    )

    permuter = (node_order[0][:, None] == jnp.arange(nodes, dtype=jnp.int32)[None, :]).astype(BF16)
    grad_columns = jnp.einsum(
        "mcg,tg->mct", grad_forecast, permuter, preferred_element_type=F32
    ).astype(BF16)
    grad_latent = jnp.einsum(
        "wc,mct->mwt", decoder_matrix, grad_columns, preferred_element_type=F32
    ).astype(BF16)
    saved = jnp.einsum("mgw,tg->mwt", hidden_embedding, permuter, preferred_element_type=F32).astype(
        BF16
    )
    split = (members, heads, width // heads, nodes)
    delta = jnp.sum(
        grad_latent.astype(F32).reshape(split) * saved.astype(F32).reshape(split), axis=2
    )
    late_own = jnp.concatenate(
        [grad_columns] + [part[n] for n in range(2) for part in (two_parts(row_lse), two_parts(delta))],
        axis=1,
    )
    late_own, own_1, before, far = lax.optimization_barrier((late_own, own_1, before, far))
    late_z = [fetched(late_own[0], "z", d) for d in (1, 2, 3)]
    late_x = [fetched(late_own[1], "x", d) for d in (1, 2, 3)]
    late_own, own_1, before = lax.optimization_barrier((late_own, own_1, before))
    after = [fetched(a, axis, 1) for a, axis in zip(own_1, ("x", "z"))]
    last = [fetched(a, axis, 3) for a, axis in zip(before, ("x", "z"))]
    came = (
        ((near[0], far[0], near[1]), (near[2], far[1], near[3])),
        ((after[0], last[0], before[0]), (after[1], last[1], before[1])),
    )

    outs = None
    parts = []
    for half in range(2):
        send_x, own, send_z = attention_tiles(
            half,
            tables,
            key_rows,
            value_rows,
            query,
            *came[half],
            late_own,
            late_x,
            late_z,
            decoder_matrix.T,
        )
        if parts:
            (first_x, first_own, first_z) = parts[0]
            send_x, send_z, first_x, first_z = lax.optimization_barrier(
                (send_x, send_z, first_x, first_z)
            )
            parts[0] = (first_x, first_own, first_z)
        got_x = lax.all_to_all(send_x, "x", 0, 0, tiled=True)
        got_z = [delivered(send_z[d - 1], "z", d) for d in (1, 2, 3)]
        parts.append((got_x, own, got_z))
    for half, part in enumerate(parts):
        outs = summed(half, *part, outs)
    grad_key, grad_value, grad_query = outs
    return grad_query, grad_key, grad_value


def solution(mesh):
    finer = Mesh(mesh.devices.reshape(4, 2, SIDE, SIDE), ("y", "core", "x", "z"))
    plane = ("x", "z")
    in_specs = (
        P(MEMBER, plane, None),
        P(),
        P(None, plane),
        P(None, plane),
        P(plane),
        P(plane, None),
        P(MEMBER, plane, None),
        P(MEMBER, plane, None),
        P(MEMBER, plane, None),
        P(MEMBER, None, plane),
        P(),
        P(),
    )
    out_specs = (P(MEMBER, plane, None), P(MEMBER, plane, None), P(MEMBER, plane, None))
    return jax.shard_map(
        shards, mesh=finer, in_specs=in_specs, out_specs=out_specs, check_vma=False
    )
```
